32 devices in a mesh: fsdp: 4 (over y, x), dp: 8 (over z, core).
Axes of the slice: x: 2, y: 2, z: 4, core: 2. Of those that a mesh axis runs over, the one named last changes fastest.
Arguments:
- tokens: bfloat16 [32, 256, 2048], P(('fsdp', 'dp')), may hold values from -6 to 6
- lengths: int32 [32], P(('fsdp', 'dp')), may hold values from 1 to 256, 5734 in all
- dealing: int32 [32], replicated, may hold values from 0 to 31, as said below
- cotangent: bfloat16 [32, 256, 2048], P(('fsdp', 'dp')), may hold values from -6 to 6
- query_weight: bfloat16 [2048, 2048], P(('fsdp', 'dp')), may hold values from -0.125 to 0.125
- key_weight: bfloat16 [2048, 2048], P(('fsdp', 'dp')), may hold values from -0.125 to 0.125
- value_weight: bfloat16 [2048, 4096], P(('fsdp', 'dp')), may hold values from -0.125 to 0.125
- gate_weight: bfloat16 [2048, 4096], P(('fsdp', 'dp')), may hold values from -0.125 to 0.125
- mixer_gain: bfloat16 [2048], P(('fsdp', 'dp')), may hold values from 0.25 to 1.75
- mixer_bias: bfloat16 [2048], P(('fsdp', 'dp')), may hold values from -1.796875 to 1.796875
- output_weight: bfloat16 [4096, 2048], P(('fsdp', 'dp')), may hold values from -0.1875 to 0.1875
- feed_gate: bfloat16 [2048, 4096], P(('fsdp', 'dp')), may hold values from -0.125 to 0.125
- feed_up: bfloat16 [2048, 4096], P(('fsdp', 'dp')), may hold values from -0.125 to 0.125
- feed_down: bfloat16 [4096, 2048], P(('fsdp', 'dp')), may hold values from -0.1875 to 0.1875
- feed_gain: bfloat16 [2048], P(('fsdp', 'dp')), may hold values from 0.25 to 1.75
- feed_bias: bfloat16 [2048], P(('fsdp', 'dp')), may hold values from -1.796875 to 1.796875
Outputs:
- out_tokens: bfloat16 [32, 256, 2048], P(('fsdp', 'dp'))
- input_grad: bfloat16 [32, 256, 2048], P(('fsdp', 'dp'))
- query_weight_grad: float32 [2048, 2048], P(('fsdp', 'dp'))
- key_weight_grad: float32 [2048, 2048], P(('fsdp', 'dp'))
- value_weight_grad: float32 [2048, 4096], P(('fsdp', 'dp'))
- gate_weight_grad: float32 [2048, 4096], P(('fsdp', 'dp'))
- mixer_gain_grad: float32 [2048], P(('fsdp', 'dp'))
- mixer_bias_grad: float32 [2048], P(('fsdp', 'dp'))
- output_weight_grad: float32 [4096, 2048], P(('fsdp', 'dp'))
- feed_gate_grad: float32 [2048, 4096], P(('fsdp', 'dp'))
- feed_up_grad: float32 [2048, 4096], P(('fsdp', 'dp'))
- feed_down_grad: float32 [4096, 2048], P(('fsdp', 'dp'))
- feed_gain_grad: float32 [2048], P(('fsdp', 'dp'))
- feed_bias_grad: float32 [2048], P(('fsdp', 'dp'))
The draws below stay inside these ranges and needn't reach their ends.
Inputs may be any that keep to these rules, and one draw needn't show every extreme that they name: dealing is a permutation of the 32 sequences; sequence s and slot dealing[s] lie on devices with the same index of dp.
All inputs are finite; a program needn't handle non-finite values. No bound on the sum of `lengths` on one device may be relied on, other than what follows from the above.
Results may differ from the reference program's by a relative error of at most 0.015.
Values may be sent and summed in bfloat16 or wider, within the bound.
No kernel may reach another device: no remote copies, remote signals or barrier semaphores. Data moves between devices by JAX's collectives and lax.ppermute only.
A program may use at most 448 MiB of HBM per device.

```python
import math
import jax
import jax.numpy as jnp
import numpy as np
from jax import lax

D = 2048
HEADS = 8
KEY = 256
VAL = 512
FF = 4096
SEQ_DEV = 1
MAXLEN = 256
VW = 4096
NSEQ = 32
N_FSDP = 4
N_DP = 8


def draw_dealing(key, part):
    group = N_FSDP * SEQ_DEV
    keys = jax.random.split(key, N_DP)
    orders = jax.vmap(lambda one_key: jax.random.permutation(one_key, group))(keys)
    outer = jnp.arange(N_FSDP)[:, None, None]
    middle = jnp.arange(N_DP)[None, :, None]
    inner = jnp.arange(SEQ_DEV)[None, None, :]
    rank_in = outer * SEQ_DEV + inner
    chosen = orders[middle, rank_in]
    slots = chosen // SEQ_DEV * (N_DP * SEQ_DEV) + middle * SEQ_DEV + chosen % SEQ_DEV
    return slots.reshape(-1).astype(jnp.int32)


def strengthened(drawn, stream_key, source, target, blocks, factor):
    owner, partner = [(jnp.arange(drawn.shape[dim]) // (drawn.shape[dim] // blocks)).reshape([-1 if axis == dim else 1 for axis in range(drawn.ndim)]) for dim in (source, target)]
    chosen = jax.random.permutation(stream_key, blocks)[partner]
    strong = (owner == chosen) | (owner == (partner + blocks // 2) % blocks)
    return jnp.where(strong, factor * drawn, drawn)


def shard_levels(key, extent, cuts, least, largest):
    factor_of, own = 1.0, jax.random.fold_in(key, 6)
    for dim, blocks in cuts:
        steps = jnp.exp(jax.random.uniform(jax.random.fold_in(own, dim), (blocks,), jnp.float32, least / len(cuts), largest / len(cuts)))
        factor_of = factor_of * jnp.repeat(steps, extent[dim] // blocks).reshape([-1 if axis == dim else 1 for axis in range(len(extent))])
    return factor_of


def split_up(number_of, total, most, lean):
    portions = [(1 << 20) // math.isqrt(rank ** lean) + 1 for rank in range(2, number_of + 1)]
    spare, counts = total - most - (number_of - 1), [1] * (number_of - 1)
    while spare > 0:
        free = [i for i in range(number_of - 1) if counts[i] < most]
        mass, left = sum([portions[i] for i in free]), spare
        for i in free:
            extra = min(most - counts[i], max(1, left * portions[i] // mass), spare)
            counts[i] = counts[i] + extra
            spare = spare - extra
    return np.array([most] + counts)


def uneven(own_key, amount, total, limit, slope):
    if amount == 2:
        one = jax.random.randint(own_key, (), max(1, total - limit), min(limit, total - 1) + 1)
        return jnp.stack([one, total - one])
    sizes = jnp.asarray(split_up(amount, total, limit, slope), jnp.int32)
    couples = (amount - 1) // 2
    source_of, receiver = sizes[1:1 + 2 * couples:2], sizes[2:2 + 2 * couples:2]
    room = jnp.minimum(source_of - 1, limit - receiver)
    shifted = jax.random.randint(jax.random.fold_in(own_key, 1), (couples,), 0, 1 << 20) % (room + 1)
    sizes = sizes.at[1:1 + 2 * couples:2].set(source_of - shifted).at[2:2 + 2 * couples:2].set(receiver + shifted)
    return sizes[jax.random.permutation(jax.random.fold_in(own_key, 2), amount)]


def gaussian(stream_key, extent, deviation, most, cuts=(), kind=jnp.bfloat16):
    entries = jax.random.normal(stream_key, extent, jnp.float32) * deviation
    if len(cuts) > 0:
        entries = shard_levels(stream_key, extent, cuts, -0.22, 0.18) * entries
    return jnp.clip(entries, min=-most, max=most).astype(kind)


def gaussian_with(key, extent, width, limit, pieces, heavy, kind=jnp.bfloat16):
    entries = width * jax.random.normal(key, extent, jnp.float32)
    if pieces:
        entries = entries * shard_levels(key, extent, pieces, -0.22, 0.18)
    return jnp.clip(strengthened(entries, jax.random.fold_in(key, 3), *heavy), -limit, limit).astype(kind)


def setup_inputs(seed: int = 0) -> dict:
    arg_keys = jax.random.split(jax.random.key(seed), 17)
    return {
        "tokens": gaussian_with(arg_keys[0], (NSEQ, MAXLEN, D), 1.0, 6.0, ((0, 32),), (0, 2, 32, 2.75)),
        "lengths": uneven(arg_keys[1], NSEQ, (7 * NSEQ * MAXLEN) // 10, MAXLEN, 1).astype(jnp.int32),
        "dealing": draw_dealing(jax.random.fold_in(arg_keys[16], 71), 0),
        "cotangent": gaussian(arg_keys[3], (NSEQ, MAXLEN, D), 1.0, 6.0, ((0, 32),)),
        "query_weight": gaussian(arg_keys[4], (D, D), D ** -0.5, 0.125, ((0, 32),)),
        "key_weight": gaussian(arg_keys[5], (D, D), D ** -0.5, 0.125, ((0, 32),)),
        "value_weight": gaussian(arg_keys[6], (D, VW), D ** -0.5, 0.125, ((0, 32),)),
        "gate_weight": gaussian(arg_keys[7], (D, VW), D ** -0.5, 0.125, ((0, 32),)),
        "mixer_gain": jnp.clip(1.0 + 0.15 * jax.random.normal(arg_keys[8], (D,), jnp.float32), 0.25, 1.75).astype(jnp.bfloat16),
        "mixer_bias": gaussian(arg_keys[9], (D,), 0.3, 1.796875, ((0, 32),)),
        "output_weight": gaussian(arg_keys[10], (VW, D), (VW // 4) ** -0.5, 0.1875, ((0, 32),)),
        "feed_gate": gaussian(arg_keys[11], (D, FF), D ** -0.5, 0.125, ((0, 32),)),
        "feed_up": gaussian(arg_keys[12], (D, FF), D ** -0.5, 0.125, ((0, 32),)),
        "feed_down": gaussian(arg_keys[13], (FF, D), (FF // 4) ** -0.5, 0.1875, ((0, 32),)),
        "feed_gain": jnp.clip(1.0 + 0.15 * jax.random.normal(arg_keys[14], (D,), jnp.float32), 0.25, 1.75).astype(jnp.bfloat16),
        "feed_bias": gaussian(arg_keys[15], (D,), 0.3, 1.796875, ((0, 32),)),
    }


EPSILON = 1e-05
RETAIN_EPSILON = 0.05
HIGH = lax.Precision.HIGHEST

@jax.custom_vjp
def low(v):
    return lax.optimization_barrier(v.astype(jnp.bfloat16)).astype(jnp.float32)

@jax.custom_vjp
def low_back(v):
    return v

def low_keep(v):
    return (low(v), None)

def low_pass(kept, grad):
    return (grad,)

def back_keep(v):
    return (v, None)

def back_low(kept, grad):
    return (low(grad),)
low.defvjp(low_keep, low_pass)
low_back.defvjp(back_keep, back_low)

def normalize_rows(field_in, offset=EPSILON):
    centre = lax.optimization_barrier(jnp.mean(field_in, axis=-1, keepdims=True))
    centred = field_in - centre
    spread = lax.optimization_barrier(jnp.mean(centred * centred, axis=-1, keepdims=True))
    return centred * lax.rsqrt(spread + offset)

def rotate(field_in, direction):
    length = field_in.shape[-3]
    breadth = field_in.shape[-1]
    half_width = breadth // 2
    columns = jnp.arange(half_width).astype(jnp.float32)
    angles = jnp.exp(-math.log(10000.0) * columns / (half_width - 1))
    zeta_scale = (2.0 * columns + 0.4 * breadth) / (1.4 * breadth)
    places = jnp.arange(length).astype(jnp.float32)[:, None]
    phases = places * angles[None, :]
    growth = jnp.exp(direction * places / 512.0 * jnp.log(zeta_scale)[None, :])
    cosine = (jnp.cos(phases) * growth)[:, None, :]
    sine_part = (jnp.sin(phases) * growth)[:, None, :]
    first_half = field_in[..., :half_width]
    second = field_in[..., half_width:]
    return jnp.concatenate([first_half * cosine - second * sine_part, second * cosine + first_half * sine_part], axis=-1)

def decay_mask(length, heads_count):
    log_decay = jnp.log(1.0 - jnp.exp2(-5.0 - jnp.arange(heads_count).astype(jnp.float32)))
    places = jnp.arange(length).astype(jnp.int32)
    distance = (places[:, None] - places[None, :]).astype(jnp.float32)
    decayed = jnp.where(distance[None] >= 0.0, jnp.exp(log_decay[:, None, None] * jnp.maximum(distance, 0.0)[None]), 0.0)
    return decayed * lax.rsqrt(lax.optimization_barrier(jnp.sum(decayed, axis=-1, keepdims=True)))

def shape_scores(raw_scores, decay):
    weighted = raw_scores * decay
    row_total = lax.optimization_barrier(jnp.sum(weighted * weighted, axis=-1, keepdims=True))
    return weighted * lax.rsqrt(1.0 + row_total)

def retnet_layer(inputs_in, live_mask, query_weight, key_weight, value_weight, gate_weight, mixer_gain, mixer_bias, output_weight, feed_gate, feed_up, feed_down, feed_gain, feed_bias):
    seq_count, length, breadth = inputs_in.shape
    mixer_normed = low(normalize_rows(inputs_in) * mixer_gain + mixer_bias)
    query_proj = low_back(jnp.einsum('nld,de->nle', mixer_normed, query_weight, precision=HIGH))
    key_proj = low_back(jnp.einsum('nld,de->nle', mixer_normed, key_weight, precision=HIGH))
    value_low = low(low_back(jnp.einsum('nld,de->nle', mixer_normed, value_weight, precision=HIGH)))
    gate_proj = low_back(jnp.einsum('nld,de->nle', mixer_normed, gate_weight, precision=HIGH))
    query_rot = low(rotate(query_proj.reshape(seq_count, length, HEADS, KEY), 1.0))
    key_rot = low(rotate(key_proj.reshape(seq_count, length, HEADS, KEY), -1.0))
    value_heads = value_low.reshape(seq_count, length, HEADS, VAL)
    raw_scores = low_back(jnp.einsum('nlhk,nmhk->nhlm', query_rot, key_rot, precision=HIGH) * KEY ** (-0.5))
    shaped = low(shape_scores(raw_scores, decay_mask(length, HEADS)))
    retained = low_back(jnp.einsum('nhlm,nmhv->nlhv', shaped, value_heads, precision=HIGH))
    gated = low(jax.nn.silu(gate_proj) * normalize_rows(retained, RETAIN_EPSILON).reshape(seq_count, length, HEADS * VAL))
    mixer_out = low_back(jnp.einsum('nle,ed->nld', gated, output_weight, precision=HIGH))
    hidden_state = inputs_in + mixer_out
    feed_normed = low(normalize_rows(hidden_state) * feed_gain + feed_bias)
    gate_pre = low_back(jnp.einsum('nld,de->nle', feed_normed, feed_gate, precision=HIGH))
    up_pre = low_back(jnp.einsum('nld,de->nle', feed_normed, feed_up, precision=HIGH))
    activated = low(jax.nn.gelu(gate_pre, approximate=False) * up_pre)
    feed_out = low_back(jnp.einsum('nle,ed->nld', activated, feed_down, precision=HIGH))
    return live_mask[:, :, None] * (hidden_state + feed_out)

def reference(tokens, lengths, dealing, cotangent, query_weight, key_weight, value_weight, gate_weight, mixer_gain, mixer_bias, output_weight, feed_gate, feed_up, feed_down, feed_gain, feed_bias):
    params = tuple((array_in.astype(jnp.float32) for array_in in (query_weight, key_weight, value_weight, gate_weight, mixer_gain, mixer_bias, output_weight, feed_gate, feed_up, feed_down, feed_gain, feed_bias)))
    per_block = math.gcd(NSEQ, max(1, 4096 // MAXLEN))
    blocks = NSEQ // per_block
    arrived = jnp.take(tokens, dealing.astype(jnp.int32), axis=0)
    inputs_all = arrived.astype(jnp.float32).reshape(blocks, per_block, MAXLEN, D)
    upstream_all = cotangent.astype(jnp.float32).reshape(blocks, per_block, MAXLEN, D)
    live_all = (jnp.arange(MAXLEN).astype(jnp.int32)[None, :] < lengths.astype(jnp.int32)[:, None]).astype(jnp.float32).reshape(blocks, per_block, MAXLEN)

    def accumulate(running, block_data):
        inputs_block, upstream_block, live_block = block_data

        def forward(inputs_in, *weights_in):
            return retnet_layer(inputs_in, live_block, *weights_in)
        result, pullback = jax.vjp(forward, inputs_block, *params)
        gradients = pullback(upstream_block)
        running = tuple((earlier + fresh for earlier, fresh in zip(running, gradients[1:])))
        return (running, (result.astype(jnp.bfloat16), gradients[0].astype(jnp.bfloat16)))
    start_totals = tuple((jnp.zeros(array_in.shape, jnp.float32) for array_in in params))
    totals, (outputs, input_grads) = lax.scan(accumulate, start_totals, (inputs_all, upstream_all, live_all))
    grads_ordered = input_grads.reshape(NSEQ, MAXLEN, D)
    input_grad = jnp.zeros(grads_ordered.shape, grads_ordered.dtype).at[dealing.astype(jnp.int32)].set(grads_ordered)
    return (outputs.reshape(NSEQ, MAXLEN, D), input_grad, totals[0], totals[1], totals[2], totals[3], totals[4], totals[5], totals[6], totals[7], totals[8], totals[9], totals[10], totals[11])
```

```python
import math

import jax
import jax.numpy as jnp
from jax import lax
from jax.sharding import Mesh, PartitionSpec as P

HEADS = 8
KEY = 256
VAL = 512
EPSILON = 1e-05
RETAIN_EPSILON = 0.05

GROUP = ("y", "x", "core")
EVERY = ("y", "x", "z", "core")
F32 = jnp.float32
BF16 = jnp.bfloat16


def normalize_rows(field_in, offset=EPSILON):
    centre = jnp.mean(field_in, axis=-1, keepdims=True)
    centred = field_in - centre
    spread = jnp.mean(centred * centred, axis=-1, keepdims=True)
    return centred * lax.rsqrt(spread + offset)


def rotate(field_in, direction):
    length = field_in.shape[-2]
    breadth = field_in.shape[-1]
    half_width = breadth // 2
    columns = jnp.arange(half_width).astype(F32)
    angles = jnp.exp(-math.log(10000.0) * columns / (half_width - 1))
    zeta_scale = (2.0 * columns + 0.4 * breadth) / (1.4 * breadth)
    places = jnp.arange(length).astype(F32)[:, None]
    phases = places * angles[None, :]
    growth = jnp.exp(direction * places / 512.0 * jnp.log(zeta_scale)[None, :])
    cosine = jnp.cos(phases) * growth
    sine_part = jnp.sin(phases) * growth
    first_half = field_in[..., :half_width]
    second = field_in[..., half_width:]
    return jnp.concatenate(
        [first_half * cosine - second * sine_part, second * cosine + first_half * sine_part],
        axis=-1,
    )


def decay_mask(length, head):
    log_decay = jnp.log(1.0 - jnp.exp2(-5.0 - head.astype(F32)))
    places = jnp.arange(length)
    distance = (places[:, None] - places[None, :]).astype(F32)
    decayed = jnp.where(distance >= 0.0, jnp.exp(log_decay * jnp.maximum(distance, 0.0)), 0.0)
    return decayed * lax.rsqrt(jnp.sum(decayed, axis=-1, keepdims=True))


def shape_scores(raw_scores, decay):
    weighted = raw_scores * decay
    row_total = jnp.sum(weighted * weighted, axis=-1, keepdims=True)
    return weighted * lax.rsqrt(1.0 + row_total)


def gate_mix(retained, gate_proj):
    return jax.nn.silu(gate_proj) * normalize_rows(retained, RETAIN_EPSILON)


def dot(left, right):
    return jnp.dot(left, right, preferred_element_type=F32)


def dot_rows(left, right):
    return lax.dot_general(left, right, (((0,), (0,)), ((), ())), preferred_element_type=F32)


def dot_back(left, right):
    return lax.dot_general(left, right, (((1,), (1,)), ((), ())), preferred_element_type=F32)


def swap(field_in, axis):
    return lax.ppermute(field_in, axis, [(0, 1), (1, 0)])


def spread_blocks(own):
    half = own.shape[0] // 2
    from_x = swap(own, "x")
    from_y = swap(own, "y")
    upper = swap(from_y[:half], "x")
    lower = swap(from_x[half:], "y")
    mine = [own, from_x, from_y, jnp.concatenate([upper, lower], axis=0)]
    blocks = []
    for block in mine:
        blocks += [block, swap(block, "core")]
    return blocks


def sum_blocks(partial):
    half = partial.shape[1] // 2
    pairs = partial.reshape(4, 2, *partial.shape[1:])
    arrived = swap(pairs[:, 1], "core")
    summed = pairs[:, 0].astype(F32) + arrived.astype(F32)
    across = summed[3].astype(BF16)
    upper = swap(across[:half], "x")
    lower = swap(across[half:], "y")
    to_y = jnp.concatenate([summed[2, :half] + upper.astype(F32), summed[2, half:]], axis=0)
    to_x = jnp.concatenate([summed[1, :half], summed[1, half:] + lower.astype(F32)], axis=0)
    from_y = swap(to_y.astype(BF16), "y")
    from_x = swap(to_x.astype(BF16), "x")
    return summed[0] + from_y.astype(F32) + from_x.astype(F32)


def body(
    tokens,
    lengths,
    dealing,
    cotangent,
    query_weight,
    key_weight,
    value_weight,
    gate_weight,
    mixer_gain,
    mixer_bias,
    output_weight,
    feed_gate,
    feed_up,
    feed_down,
    feed_gain,
    feed_bias,
):
    _, length, breadth = tokens.shape
    layers = lax.axis_size("z")
    local_model = query_weight.shape[0]
    local_hidden = feed_down.shape[0]
    local_value = output_weight.shape[0]
    group = 8
    half_layers = layers // 2
    hidden = local_hidden * layers
    scale_factor = KEY ** (-0.5)
    fsdp_index = lax.axis_index("y") * 2 + lax.axis_index("x")
    core = lax.axis_index("core")
    layer = lax.axis_index("z")
    head = fsdp_index * 2 + core

    def across_group(packed):
        return lax.all_to_all(packed, GROUP, 0, 0, tiled=True)

    def gather_layers(packed):
        width = packed.shape[-1]
        return lax.all_gather(
            packed.reshape(4, 2 * local_model, width), "z", axis=1, tiled=True
        ).reshape(-1, width)

    def value_columns(weight):
        split = weight.reshape(local_model, 4, 2, half_layers, 2, local_value)
        return split.transpose(1, 2, 0, 4, 3, 5).reshape(group, local_model, VAL)

    def hidden_columns(weight):
        split = weight.reshape(local_model, 4, layers, 2, local_hidden)
        return split.transpose(1, 3, 0, 2, 4).reshape(group, local_model, hidden)

    def head_columns(weight):
        return weight.reshape(local_model, group, KEY).transpose(1, 0, 2)

    mixer_packed = jnp.concatenate(
        [
            head_columns(query_weight),
            head_columns(key_weight),
            value_columns(value_weight),
            value_columns(gate_weight),
        ],
        axis=2,
    )
    mixer_weight = gather_layers(across_group(mixer_packed))
    features = lax.all_gather(
        jnp.stack([mixer_gain, mixer_bias, feed_gain, feed_bias]), EVERY, axis=1, tiled=True
    ).astype(F32)
    out_weight = lax.all_gather(output_weight, "z", axis=0, tiled=True)
    out_weight = lax.all_to_all(out_weight, "core", 0, 0, tiled=True)
    feed_packed = jnp.concatenate([hidden_columns(feed_gate), hidden_columns(feed_up)], axis=2)
    feed_weight = gather_layers(across_group(feed_packed))
    down_weight = lax.all_gather(feed_down, "z", axis=0, tiled=True)

    def slot_of(bits_f, bits_c):
        member_f = fsdp_index ^ bits_f
        member_c = core ^ bits_c
        number = (member_f * layers + layer) * 2 + member_c
        return (fsdp_index ^ (dealing[number] // (2 * layers))) * 2 + bits_c

    to_slot = jnp.stack([slot_of(j // 2, j % 2) for j in range(group)])
    own_number = (fsdp_index * layers + layer) * 2 + core
    back_f = jnp.int32(0)
    for bits in range(4):
        back_f = jnp.where(to_slot[bits * 2] == 0, bits, back_f)
    own_sequence = back_f * 2
    slots = jnp.arange(group, dtype=jnp.int32)
    to_sequence = jnp.sum(
        jnp.where(to_slot[None, :] == slots[:, None], slots[None, :], 0), axis=1
    )

    token_blocks = spread_blocks(tokens[0])
    token_all = jnp.stack(token_blocks)
    residual_in = lax.dynamic_index_in_dim(token_all, to_slot[0], 0, keepdims=False).astype(F32)
    mixer_normed = (
        normalize_rows(token_all.astype(F32)) * features[0] + features[1]
    ).astype(BF16).reshape(group * length, breadth)

    places = jnp.arange(length, dtype=jnp.int32)
    live_mask = (places < lengths[0]).astype(F32)[:, None]
    upstream = cotangent[0].astype(F32) * live_mask
    down_low = jnp.stack(spread_blocks(upstream.astype(BF16))).reshape(group * length, breadth)

    projected = dot(mixer_normed, mixer_weight).reshape(group, length, -1)
    queries = projected[..., :KEY]
    key_proj = projected[..., KEY : 2 * KEY]
    value_low = projected[..., 2 * KEY : 2 * KEY + VAL].astype(BF16)
    gate_proj = projected[..., 2 * KEY + VAL :]
    query_rot, query_pull = jax.vjp(lambda field_in: rotate(field_in, 1.0), queries)
    key_rot, key_pull = jax.vjp(lambda field_in: rotate(field_in, -1.0), key_proj)
    query_low = query_rot.astype(BF16)
    key_low = key_rot.astype(BF16)
    decay = decay_mask(length, head)
    raw_scores = (
        jnp.einsum("nlk,nmk->nlm", query_low, key_low, preferred_element_type=F32) * scale_factor
    )
    shaped, shape_pull = jax.vjp(lambda scores_in: shape_scores(scores_in, decay), raw_scores)
    shaped_low = shaped.astype(BF16)
    retained = jnp.einsum("nlm,nmv->nlv", shaped_low, value_low, preferred_element_type=F32)
    gated_full, gate_pull = jax.vjp(gate_mix, retained, gate_proj)
    gated_low = jnp.take(gated_full.astype(BF16), to_slot, axis=0).reshape(group * length, VAL)

    mixer_part = dot(gated_low, out_weight).astype(BF16).reshape(group, length, breadth)
    hidden_state = residual_in + sum_blocks(mixer_part)
    feed_hat, feed_pull = jax.vjp(normalize_rows, hidden_state)
    own_normed = (feed_hat * features[2] + features[3]).astype(BF16)
    feed_normed = jnp.stack(spread_blocks(own_normed)).reshape(group * length, breadth)

    feed_pre = dot(feed_normed, feed_weight)
    gate_pre = feed_pre[:, :hidden]
    up_pre = feed_pre[:, hidden:]
    activated_full, act_pull = jax.vjp(
        lambda gate_in, up_in: jax.nn.gelu(gate_in, approximate=False) * up_in, gate_pre, up_pre
    )
    activated = activated_full.astype(BF16)
    feed_part = dot(activated, down_weight).astype(BF16).reshape(group, length, breadth)

    act_grad = dot_back(down_low, down_weight)
    gate_pre_grad, up_pre_grad = act_pull(act_grad)
    pre_low = jnp.concatenate([gate_pre_grad.astype(BF16), up_pre_grad.astype(BF16)], axis=1)
    normed_part = dot_back(pre_low, feed_weight).astype(BF16).reshape(group, length, breadth)
    feed_normed_grad = sum_blocks(normed_part)
    feed_gain_part = jnp.sum(feed_normed_grad * feed_hat, axis=0)
    feed_bias_part = jnp.sum(feed_normed_grad, axis=0)
    state_grad = upstream + feed_pull(feed_normed_grad * features[2])[0]
    own_grad_low = state_grad.astype(BF16)
    out_grad_blocks = jnp.stack(spread_blocks(own_grad_low))
    out_grad_low = out_grad_blocks.reshape(group * length, breadth)

    out_tokens = (live_mask * (hidden_state + sum_blocks(feed_part))).astype(BF16)

    def scatter_layers(grads):
        width = grads.shape[-1]
        return lax.psum_scatter(
            grads.astype(BF16).reshape(4, -1, width), "z", scatter_dimension=1, tiled=True
        ).reshape(group, local_model, width)

    down_grad = lax.psum_scatter(
        dot_rows(activated, down_low).astype(BF16), "z", scatter_dimension=0, tiled=True
    ).astype(F32)
    feed_grads = across_group(scatter_layers(dot_rows(feed_normed, pre_low))).astype(F32)

    gated_grad = jnp.take(
        dot_back(out_grad_low, out_weight).reshape(group, length, VAL), to_sequence, axis=0
    )
    out_weight_grad = dot_rows(gated_low, out_grad_low).astype(BF16)
    out_weight_grad = lax.all_to_all(out_weight_grad, "core", 0, 0, tiled=True)
    output_grad = lax.psum_scatter(out_weight_grad, "z", scatter_dimension=0, tiled=True).astype(F32)

    retained_grad, gate_proj_grad = gate_pull(gated_grad)
    retained_low = retained_grad.astype(BF16)
    value_grad = jnp.einsum("nlm,nlv->nmv", shaped_low, retained_low, preferred_element_type=F32)
    shaped_grad = jnp.einsum("nlv,nmv->nlm", retained_low, value_low, preferred_element_type=F32)
    score_grad = shape_pull(shaped_grad)[0].astype(BF16)
    query_rot_grad = (
        jnp.einsum("nlm,nmk->nlk", score_grad, key_low, preferred_element_type=F32) * scale_factor
    )
    key_rot_grad = (
        jnp.einsum("nlm,nlk->nmk", score_grad, query_low, preferred_element_type=F32) * scale_factor
    )
    mixer_grad_low = jnp.concatenate(
        [
            query_pull(query_rot_grad)[0].astype(BF16),
            key_pull(key_rot_grad)[0].astype(BF16),
            value_grad.astype(BF16),
            gate_proj_grad.astype(BF16),
        ],
        axis=2,
    ).reshape(group * length, -1)
    mixer_grads = across_group(scatter_layers(dot_rows(mixer_normed, mixer_grad_low))).astype(F32)
    mixer_part_grad = dot_back(mixer_grad_low, mixer_weight).astype(BF16)
    mixer_normed_grad = sum_blocks(mixer_part_grad.reshape(group, length, breadth))
    mixer_hat, mixer_pull = jax.vjp(normalize_rows, tokens[0].astype(F32))
    mixer_gain_part = jnp.sum(mixer_normed_grad * mixer_hat, axis=0)
    mixer_bias_part = jnp.sum(mixer_normed_grad, axis=0)
    slot_grad = lax.dynamic_index_in_dim(out_grad_blocks, own_sequence, 0, keepdims=False)
    input_grad = (
        slot_grad.astype(F32) + mixer_pull(mixer_normed_grad * features[0])[0]
    ).astype(BF16)

    feature_grads = lax.psum_scatter(
        jnp.stack([mixer_gain_part, mixer_bias_part, feed_gain_part, feed_bias_part]),
        EVERY,
        scatter_dimension=1,
        tiled=True,
    )

    def head_back(grads):
        return grads.transpose(1, 0, 2).reshape(local_model, -1)

    def value_back(grads):
        split = grads.reshape(4, 2, local_model, 2, half_layers, local_value)
        return split.transpose(2, 0, 1, 4, 3, 5).reshape(local_model, -1)

    def hidden_back(grads):
        split = grads.reshape(4, 2, local_model, layers, local_hidden)
        return split.transpose(2, 0, 3, 1, 4).reshape(local_model, -1)

    return (
        out_tokens[None],
        input_grad[None],
        head_back(mixer_grads[..., :KEY]),
        head_back(mixer_grads[..., KEY : 2 * KEY]),
        value_back(mixer_grads[..., 2 * KEY : 2 * KEY + VAL]),
        value_back(mixer_grads[..., 2 * KEY + VAL :]),
        feature_grads[0],
        feature_grads[1],
        output_grad,
        hidden_back(feed_grads[..., :hidden]),
        hidden_back(feed_grads[..., hidden:]),
        down_grad,
        feature_grads[2],
        feature_grads[3],
    )


def solution(mesh):
    layers = mesh.shape["dp"] // 2
    fine = Mesh(mesh.devices.reshape(2, 2, layers, 2), EVERY)
    sequences = P(EVERY, None, None)
    rows = P(EVERY, None)
    vector = P(EVERY)
    in_specs = (
        (sequences, vector, P(), sequences)
        + (rows,) * 4
        + (vector,) * 2
        + (rows,) * 4
        + (vector,) * 2
    )
    out_specs = (
        (sequences,) * 2 + (rows,) * 4 + (vector,) * 2 + (rows,) * 4 + (vector,) * 2
    )
    return jax.shard_map(body, mesh=fine, in_specs=in_specs, out_specs=out_specs, check_vma=False)
```

```python
import math

import jax
import jax.numpy as jnp
from jax import lax
from jax.experimental import pallas as pl
from jax.experimental.pallas import tpu as pltpu
from jax.sharding import Mesh, PartitionSpec as P

HEADS = 8
KEY = 256
VAL = 512
EPSILON = 1e-05
RETAIN_EPSILON = 0.05
SCALE = KEY ** (-0.5)

EVERY = ("y", "x", "z", "core")
MEMBERS = ("y", "x", "core")
GROUP = 8
F32 = jnp.float32
BF16 = jnp.bfloat16


def dot(left, right):
    return jnp.dot(left, right, preferred_element_type=F32)


def dot_rows(left, right):
    return lax.dot_general(left, right, (((0,), (0,)), ((), ())), preferred_element_type=F32)


def dot_back(left, right):
    return lax.dot_general(left, right, (((1,), (1,)), ((), ())), preferred_element_type=F32)


def statistics(field_in, offset):
    centred = field_in - jnp.mean(field_in, axis=-1, keepdims=True)
    inverse = lax.rsqrt(jnp.mean(centred * centred, axis=-1, keepdims=True) + offset)
    return centred * inverse, inverse


def pull_back(hat, inverse, grad):
    return inverse * (
        grad
        - jnp.mean(grad, axis=-1, keepdims=True)
        - hat * jnp.mean(grad * hat, axis=-1, keepdims=True)
    )


def rotation_tables(length):
    half_width = KEY // 2
    columns = jnp.arange(half_width).astype(F32)
    angles = jnp.exp(-math.log(10000.0) * columns / (half_width - 1))
    zeta_scale = (2.0 * columns + 0.4 * KEY) / (1.4 * KEY)
    places = jnp.arange(length).astype(F32)[:, None]
    phases = places * angles[None, :]
    tables = []
    for direction in (1.0, -1.0):
        growth = jnp.exp(direction * places / 512.0 * jnp.log(zeta_scale)[None, :])
        tables += [jnp.cos(phases) * growth, jnp.sin(phases) * growth]
    return jnp.stack(tables)


def decay_mask(length, head):
    log_decay = jnp.log(1.0 - jnp.exp2(-5.0 - head.astype(F32)))
    places = jnp.arange(length)
    distance = (places[:, None] - places[None, :]).astype(F32)
    decayed = jnp.where(distance >= 0.0, jnp.exp(log_decay * jnp.maximum(distance, 0.0)), 0.0)
    return decayed * lax.rsqrt(jnp.sum(decayed, axis=-1, keepdims=True))


def read_rows(refs):
    return jnp.concatenate([ref[...] for ref in refs], axis=0) if len(refs) > 1 else refs[0][...]


def turn(field_in, cosine, sine):
    first, second = field_in[:, : KEY // 2], field_in[:, KEY // 2 :]
    return jnp.concatenate([first * cosine - second * sine, second * cosine + first * sine], axis=1)


def turn_back(field_in, cosine, sine):
    first, second = field_in[:, : KEY // 2], field_in[:, KEY // 2 :]
    return jnp.concatenate([first * cosine + second * sine, second * cosine - first * sine], axis=1)


def whole_spec(array):
    zeros = (0,) * array.ndim
    return pl.BlockSpec(array.shape, lambda i: zeros, pipeline_mode=pl.Buffered(1))


def pair_spec(shape, number):
    return pl.BlockSpec((2,) + shape, lambda i: (number,) + (0,) * len(shape))


def chunk_call(body_fn, name, number, pieces, shared, saved_in, buffers, shapes, parts, flops, tokens=()):
    flat = [piece for side in pieces for piece in side]
    counts = [len(side) for side in pieces]
    total = len(flat) + len(shared) + len(saved_in)
    carried = [] if buffers is None else list(buffers)

    def kernel(*refs):
        sides, at = [], 0
        for count in counts:
            sides.append(refs[at : at + count])
            at += count
        body_fn(sides, refs[at : at + len(shared)], refs[at + len(shared) : total], refs[total + len(carried) + len(tokens) :])

    outs = [jax.ShapeDtypeStruct((GROUP,) + shape, dtype) for shape, dtype in shapes]
    outs += [jax.ShapeDtypeStruct(shape, dtype) for shape, dtype in parts]
    operands = [*flat, *shared, *saved_in, *carried, *tokens]
    size = sum(math.prod(o.shape) * o.dtype.itemsize for o in [*flat, *shared])
    return pl.pallas_call(
        kernel,
        grid=(1,),
        out_shape=outs,
        in_specs=[whole_spec(o) for o in [*flat, *shared]]
        + [pair_spec(o.shape[1:], number) for o in saved_in]
        + [pl.BlockSpec(memory_space=pl.ANY) for _ in [*carried, *tokens]],
        out_specs=[pair_spec(shape, number) for shape, _ in shapes]
        + [pl.BlockSpec(shape, lambda i: (0, 0)) for shape, _ in parts],
        input_output_aliases={total + i: i for i in range(len(carried))},
        compiler_params=pltpu.CompilerParams(vmem_limit_bytes=56 * 1024 * 1024),
        cost_estimate=pl.CostEstimate(flops=flops, bytes_accessed=size, transcendentals=0),
        name=name,
    )(*operands)


def mixer_forward(sides, shared, saved_in, outs):
    features, tables, decay, weight, weight_o = shared
    normed_out, qkv_out, gate_out, gated_out = outs[:4]
    parts = outs[4:]
    cos_q, sin_q, cos_k, sin_k = (tables[i] for i in range(4))
    for s, side in enumerate(sides):
        hat, _ = statistics(read_rows(side).astype(F32), EPSILON)
        normed = (hat * features[0:1, :] + features[1:2, :]).astype(BF16)
        normed_out[s] = normed
        projected = dot(normed, weight[...])
        query_low = turn(projected[:, :KEY], cos_q, sin_q).astype(BF16)
        key_low = turn(projected[:, KEY : 2 * KEY], cos_k, sin_k).astype(BF16)
        value_low = projected[:, 2 * KEY : 2 * KEY + VAL].astype(BF16)
        gate = projected[:, 2 * KEY + VAL :]
        weighted = dot_back(query_low, key_low) * SCALE * decay[...]
        shaped = weighted * lax.rsqrt(1.0 + jnp.sum(weighted * weighted, axis=-1, keepdims=True))
        retained = dot(shaped.astype(BF16), value_low)
        retained_hat, _ = statistics(retained, RETAIN_EPSILON)
        qkv_out[s, :, :KEY] = query_low
        qkv_out[s, :, KEY : 2 * KEY] = key_low
        qkv_out[s, :, 2 * KEY :] = value_low
        gate_out[s] = gate
        gated = (gate * jax.nn.sigmoid(gate) * retained_hat).astype(BF16)
        gated_out[s] = gated
        parts[s][...] = dot(gated, weight_o[...]).astype(BF16)


def mixer_backward(sides, shared, saved_in, outs):
    tables, decay_ref, weight, weight_o = shared
    qkv, gate_ref = saved_in
    og_out, qk_out, vg_out = outs[:3]
    parts = outs[3:]
    cos_q, sin_q, cos_k, sin_k = (tables[i] for i in range(4))
    decay = decay_ref[...]
    for s, side in enumerate(sides):
        out_grad = read_rows(side)
        og_out[s] = out_grad
        gated_grad = dot_back(out_grad, weight_o[...])
        query_low = qkv[s, :, :KEY]
        key_low = qkv[s, :, KEY : 2 * KEY]
        value_low = qkv[s, :, 2 * KEY :]
        weighted = dot_back(query_low, key_low) * SCALE * decay
        inverse_c = lax.rsqrt(1.0 + jnp.sum(weighted * weighted, axis=-1, keepdims=True))
        shaped_low = (weighted * inverse_c).astype(BF16)
        retained_hat, inverse = statistics(dot(shaped_low, value_low), RETAIN_EPSILON)
        gate = gate_ref[s]
        sig = jax.nn.sigmoid(gate)
        gate_grad = (gated_grad * retained_hat * (sig * (1.0 + gate * (1.0 - sig)))).astype(BF16)
        retained_low = pull_back(retained_hat, inverse, gated_grad * (gate * sig)).astype(BF16)
        value_grad = dot_rows(shaped_low, retained_low).astype(BF16)
        shaped_grad = dot_back(retained_low, value_low)
        row_sum = jnp.sum(shaped_grad * weighted, axis=-1, keepdims=True)
        cubed = inverse_c * inverse_c * inverse_c
        score_grad = (decay * (shaped_grad * inverse_c - weighted * (row_sum * cubed))).astype(BF16)
        query_grad = turn_back(dot(score_grad, key_low) * SCALE, cos_q, sin_q).astype(BF16)
        key_grad = turn_back(dot_rows(score_grad, query_low) * SCALE, cos_k, sin_k).astype(BF16)
        both = jnp.concatenate([query_grad, key_grad], axis=1)
        value_gate = jnp.concatenate([value_grad, gate_grad], axis=1)
        qk_out[s] = both
        vg_out[s] = value_gate
        parts[s][...] = dot_back(jnp.concatenate([both, value_gate], axis=1), weight[...]).astype(BF16)


def feed_forward(sides, shared, saved_in, outs):
    (weight,) = shared
    normed_out, act_out, slopes_out, done = outs
    hidden = act_out.shape[2]
    done[...] = jnp.zeros_like(done)
    for s, side in enumerate(sides):
        normed = read_rows(side)
        normed_out[s] = normed
        pre = dot(normed, weight[...])
        gate_pre, up_pre = pre[:, :hidden], pre[:, hidden:]
        phi = 0.5 * (1.0 + lax.erf(gate_pre * math.sqrt(0.5)))
        gelu = gate_pre * phi
        slope = phi + gate_pre * (jnp.exp(-0.5 * gate_pre * gate_pre) * (1.0 / math.sqrt(2.0 * math.pi)))
        act_out[s] = (gelu * up_pre).astype(BF16)
        slopes_out[s, :, :hidden] = up_pre * slope
        slopes_out[s, :, hidden:] = gelu


def feed_backward(sides, shared, saved_in, outs):
    weight, down = shared
    act_ref, slopes, upstream_ref = saved_in
    pre_out = outs[0]
    feed_parts, normed_parts = outs[1:3], outs[3:5]
    for s in range(2):
        act_grad = dot_back(upstream_ref[s], down[...])
        low = (jnp.concatenate([act_grad, act_grad], axis=1) * slopes[s]).astype(BF16)
        pre_out[s] = low
        normed_parts[s][...] = dot_back(low, weight[...]).astype(BF16)
        feed_parts[s][...] = dot(act_ref[s], down[...]).astype(BF16)


def swap(field_in, axis):
    return lax.ppermute(field_in, axis, [(0, 1), (1, 0)])


def swap_both(field_in, axes):
    return lax.ppermute(field_in, axes, [(0, 3), (1, 2), (2, 1), (3, 0)])


def after(values, *tokens):
    anywhere = pl.BlockSpec(memory_space=pl.ANY)
    held = pl.pallas_call(
        lambda *refs: None,
        out_shape=[jax.ShapeDtypeStruct(v.shape, v.dtype) for v in values],
        in_specs=[anywhere] * (len(values) + len(tokens)),
        out_specs=[anywhere] * len(values),
        input_output_aliases={i: i for i in range(len(values))},
        cost_estimate=pl.CostEstimate(flops=0, bytes_accessed=0, transcendentals=0),
        name="after",
    )(*values, *tokens)
    return list(held)


def pair_up(pieces):
    return pieces, [swap(piece, "core") for piece in pieces]


def spread(own):
    half = own.shape[0] // 2
    from_x = swap(own, "x")
    from_y = swap(own, "y")
    upper = swap(from_y[:half], "x")
    lower = swap(from_x[half:], "y")
    return [pair_up(pieces) for pieces in ([own], [from_x], [from_y], [upper, lower])]


def chunks_in_turn(own, call):
    half = own.shape[0] // 2
    from_x = swap(own, "x")
    from_y = swap(own, "y")
    results = [call(0, pair_up([own]), [])]
    from_x, from_y = after([from_x, from_y], results[0][-1])
    upper = swap(from_y[:half], "x")
    lower = swap(from_x[half:], "y")
    chunk_x, chunk_y = pair_up([from_x]), pair_up([from_y])
    results.append(call(1, chunk_x, results))
    across = after([upper, lower], results[1][-1])
    chunk_across = pair_up(across)
    results.append(call(2, chunk_y, results))
    results.append(call(3, chunk_across, results))
    return results


def two_cores(pair):
    return pair[0].astype(F32) + swap(pair[1], "core").astype(F32)


def send(number, summed):
    summed = summed.astype(BF16)
    if number == 3:
        return swap_both(summed, ("y", "x"))
    return swap(summed, ("x", "y")[number - 1])


def add_up(own, arrived):
    return own + arrived[1].astype(F32) + arrived[2].astype(F32) + arrived[3].astype(F32)


def body(
    tokens,
    lengths,
    dealing,
    cotangent,
    query_weight,
    key_weight,
    value_weight,
    gate_weight,
    mixer_gain,
    mixer_bias,
    output_weight,
    feed_gate,
    feed_up,
    feed_down,
    feed_gain,
    feed_bias,
):
    _, length, breadth = tokens.shape
    layers = lax.axis_size("z")
    devices = 8 * layers
    local_model = query_weight.shape[0]
    local_hidden = feed_down.shape[0]
    local_value = output_weight.shape[0]
    hidden = local_hidden * layers
    half_layers = layers // 2
    fsdp_index = lax.axis_index("y") * 2 + lax.axis_index("x")
    core = lax.axis_index("core")
    layer = lax.axis_index("z")
    head = fsdp_index * 2 + core

    def to_members(packed, axes=MEMBERS):
        return lax.all_to_all(packed, axes, 0, 0, tiled=True)

    def gather_layers(mine):
        return lax.all_gather(
            mine.reshape(4, 2 * local_model, -1), "z", axis=1, tiled=True
        ).reshape(breadth, -1)

    def value_columns(weight):
        split = weight.reshape(local_model, 4, 2, half_layers, 2, local_value)
        return split.transpose(1, 2, 0, 4, 3, 5).reshape(GROUP, local_model, VAL)

    def head_columns(weight):
        return weight.reshape(local_model, HEADS, KEY).transpose(1, 0, 2)

    def hidden_columns(weight):
        split = weight.reshape(local_model, 4, layers, 2, local_hidden)
        return split.transpose(1, 3, 0, 2, 4).reshape(GROUP, local_model, hidden)

    weight_o = lax.all_gather(output_weight, "z", axis=0, tiled=True)
    mixer_mine = to_members(
        jnp.concatenate(
            [
                head_columns(query_weight),
                head_columns(key_weight),
                value_columns(value_weight),
                value_columns(gate_weight),
            ],
            axis=2,
        )
    )
    mixer_weight = gather_layers(mixer_mine)
    feed_packed = jnp.concatenate([hidden_columns(feed_gate), hidden_columns(feed_up)], axis=2)
    feed_mine = to_members(feed_packed)
    feed_weight = gather_layers(feed_mine)
    down_weight = lax.all_gather(feed_down, "z", axis=0, tiled=True)
    weight_o = to_members(weight_o, "core")

    vectors = jnp.stack([mixer_gain, mixer_bias, feed_gain, feed_bias])
    features = to_members(jnp.broadcast_to(vectors[None], (devices,) + vectors.shape), EVERY)
    features = features.transpose(1, 0, 2).reshape(4, breadth).astype(F32)

    slot_bits = []
    for bits_c in range(2):
        numbers = [
            ((fsdp_index ^ bits_f) * layers + layer) * 2 + (core ^ bits_c) for bits_f in range(4)
        ]
        slot_bits.append([fsdp_index ^ (dealing[n] // (2 * layers)) for n in numbers])
    sequence_in = []
    for slot in range(4):
        for bits_c in range(2):
            found = jnp.int32(0)
            for bits_f in range(1, 4):
                found = jnp.where(slot_bits[bits_c][bits_f] == slot, bits_f, found)
            sequence_in.append(found * 2 + bits_c)
    own_slot = slot_bits[0][0]

    places = jnp.arange(length, dtype=jnp.int32)
    live_mask = (places < lengths[0]).astype(F32)[:, None]
    upstream_own = (cotangent[0].astype(F32) * live_mask).astype(BF16)
    upstream_blocks = jnp.stack(
        [read for chunk in spread(upstream_own) for read in map(join, chunk)]
    )
    upstream_all = jnp.stack(
        [lax.dynamic_index_in_dim(upstream_blocks, n, 0, keepdims=False) for n in sequence_in]
    )

    tables = rotation_tables(length)
    decay = decay_mask(length, head)
    row_bytes = (length, breadth)
    saved, summed, arrived = None, [None] * 4, [None] * 4
    token_chunks = spread(tokens[0])
    order = (3, 1, 2, 0)
    for i, n in enumerate(order):
        results = chunk_call(
            mixer_forward,
            "mixer_forward",
            n,
            token_chunks[n],
            [features[:2], tables, decay, mixer_weight, weight_o],
            [],
            saved,
            [
                ((length, breadth), BF16),
                ((length, 2 * KEY + VAL), BF16),
                ((length, VAL), F32),
                ((length, VAL), BF16),
            ],
            [(row_bytes, BF16)] * 2,
            2 * 2 * length * breadth * 2048,
            [upstream_all] if i < 2 else [summed[order[i - 2]]],
        )
        saved = results[:4]
        summed[n] = two_cores(results[4:6])
        arrived[n] = send(n, summed[n]) if n else None
    mixer_normed, qkv_all, gate_all, gated_all = saved
    arrived[3] = after([arrived[3]], feed_weight)[0]
    hidden_state = tokens[0].astype(F32) + add_up(summed[0], arrived)

    feed_hat, feed_inverse = statistics(hidden_state, EPSILON)
    feed_own = (feed_hat * features[2] + features[3]).astype(BF16)

    def feed_call(n, chunk, earlier):
        return chunk_call(
            feed_forward,
            "feed_forward",
            n,
            chunk,
            [feed_weight],
            [],
            earlier[-1][:3] if earlier else None,
            [((length, breadth), BF16), ((length, hidden), BF16), ((length, 2 * hidden), F32)],
            [((8, 128), F32)],
            2 * 2 * length * breadth * hidden * 2,
            [down_weight] if n == 3 else [],
        )

    saved = chunks_in_turn(feed_own, feed_call)[-1][:3]
    feed_normed, activated, slopes = saved
    down_product = dot_rows(
        activated.reshape(GROUP * length, hidden), upstream_all.reshape(GROUP * length, breadth)
    ).astype(BF16)
    down_grad = lax.psum_scatter(down_product, "z", scatter_dimension=0, tiled=True)

    saved, summed, arrived, feed_parts = None, [None] * 4, [None] * 4, [None] * 4
    for i, n in enumerate(order):
        results = chunk_call(
            feed_backward,
            "feed_backward",
            n,
            [],
            [feed_weight, down_weight],
            [activated, slopes, upstream_all],
            saved,
            [((length, 2 * hidden), BF16)],
            [(row_bytes, BF16)] * 4,
            2 * 2 * length * breadth * hidden * 4,
            [down_product] if i < 2 else [summed[order[i - 2]]],
        )
        saved = results[:1]
        feed_parts[n] = results[1:3]
        summed[n] = two_cores(results[3:5])
        arrived[n] = send(n, summed[n]) if n else None
    feed_product = dot_rows(
        feed_normed.reshape(GROUP * length, breadth),
        saved[0].reshape(GROUP * length, -1),
    ).astype(BF16)
    arrived = [None] + after(arrived[1:], feed_product, down_grad)
    feed_normed_grad = add_up(summed[0], arrived)
    feed_gain_part = jnp.sum(feed_normed_grad * feed_hat, axis=0)
    feed_bias_part = jnp.sum(feed_normed_grad, axis=0)
    state_grad = upstream_all[0].astype(F32) + pull_back(
        feed_hat, feed_inverse, feed_normed_grad * features[2]
    )
    own_grad_low = state_grad.astype(BF16)

    def sum_layers(grads):
        return lax.psum_scatter(
            grads.reshape(4, -1, grads.shape[-1]), "z", scatter_dimension=1, tiled=True
        )

    def to_owners(mine):
        return to_members(mine.reshape(GROUP, local_model, -1)).astype(F32)

    feed_summed = sum_layers(feed_product)
    feed_grads = to_owners(feed_summed)

    summed, grad_parts = [None] * 4, [None] * 4

    def backward_call(n, chunk, earlier):
        if n == 3:
            summed[1] = two_cores(earlier[1][3:5])
        return chunk_call(
            mixer_backward,
            "mixer_backward",
            n,
            chunk,
            [tables, decay, mixer_weight, weight_o],
            [qkv_all, gate_all],
            earlier[-1][:3] if earlier else None,
            [((length, breadth), BF16), ((length, 2 * KEY), BF16), ((length, 2 * VAL), BF16)],
            [(row_bytes, BF16)] * 2,
            2 * 2 * length * breadth * 2304,
            [summed[1], feed_summed] if n == 3 else [],
        )

    results = chunks_in_turn(own_grad_low, backward_call)
    saved = results[-1][:3]
    grad_parts = [result[3:5] for result in results]
    summed = [summed[1] if n == 1 else two_cores(grad_parts[n]) for n in range(4)]
    arrived = [None] + [send(n, summed[n]) for n in range(1, 4)]
    out_grad, qk_grad, vg_grad = (a.reshape(GROUP * length, -1) for a in saved)

    normed_rows = mixer_normed.reshape(GROUP * length, breadth)
    qk_product = dot_rows(normed_rows, qk_grad).astype(BF16)
    vg_product = dot_rows(normed_rows, vg_grad).astype(BF16)
    out_product = dot_rows(gated_all.reshape(GROUP * length, VAL), out_grad).astype(BF16)
    qk_grads = to_owners(sum_layers(qk_product))
    vg_grads = to_owners(sum_layers(vg_product))
    output_grad = lax.psum_scatter(
        to_members(out_product, "core"), "z", scatter_dimension=0, tiled=True
    ).astype(F32)

    held = after([part for pair in feed_parts for part in pair], grad_parts[1][0])
    feed_parts = [held[2 * n : 2 * n + 2] for n in range(4)]
    feed_terms = [two_cores(pair) for pair in feed_parts]
    feed_arrived = [None] + after([send(n, feed_terms[n]) for n in range(1, 4)], out_product)
    slot_out = (hidden_state + add_up(feed_terms[0], feed_arrived)).astype(BF16)
    half = length // 2
    from_x, from_y = swap(slot_out, "x"), swap(slot_out, "y")
    across = jnp.concatenate([swap(from_y[:half], "x"), swap(from_x[half:], "y")], axis=0)
    reached = jnp.stack([slot_out, from_x, from_y, across])
    chosen = lax.dynamic_index_in_dim(reached, own_slot, 0, keepdims=False)
    out_tokens = (live_mask * chosen.astype(F32)).astype(BF16)

    arrived = [None] + after(arrived[1:], out_product)
    mixer_normed_grad = add_up(summed[0], arrived)
    mixer_hat, mixer_inverse = statistics(tokens[0].astype(F32), EPSILON)
    mixer_gain_part = jnp.sum(mixer_normed_grad * mixer_hat, axis=0)
    mixer_bias_part = jnp.sum(mixer_normed_grad, axis=0)
    input_grad = (
        state_grad + pull_back(mixer_hat, mixer_inverse, mixer_normed_grad * features[0])
    ).astype(BF16)

    def vector_grads(*grads):
        split = jnp.stack(grads).reshape(len(grads), devices, -1).transpose(1, 0, 2)
        return jnp.sum(to_members(split, EVERY), axis=0)

    feed_vectors = vector_grads(feed_gain_part, feed_bias_part)
    mixer_vectors = vector_grads(mixer_gain_part, mixer_bias_part)

    def head_back(grads):
        return grads.transpose(1, 0, 2).reshape(local_model, -1)

    def value_back(grads):
        split = grads.reshape(4, 2, local_model, 2, half_layers, local_value)
        return split.transpose(2, 0, 1, 4, 3, 5).reshape(local_model, -1)

    def hidden_back(grads):
        split = grads.reshape(4, 2, local_model, layers, local_hidden)
        return split.transpose(2, 0, 3, 1, 4).reshape(local_model, -1)

    return (
        out_tokens[None],
        input_grad[None],
        head_back(qk_grads[..., :KEY]),
        head_back(qk_grads[..., KEY:]),
        value_back(vg_grads[..., :VAL]),
        value_back(vg_grads[..., VAL:]),
        mixer_vectors[0],
        mixer_vectors[1],
        output_grad,
        hidden_back(feed_grads[..., :hidden]),
        hidden_back(feed_grads[..., hidden:]),
        down_grad.astype(F32),
        feed_vectors[0],
        feed_vectors[1],
    )


def join(pieces):
    return jnp.concatenate(pieces, axis=0) if len(pieces) > 1 else pieces[0]


def solution(mesh):
    layers = mesh.shape["dp"] // 2
    fine = Mesh(mesh.devices.reshape(2, 2, layers, 2), EVERY)
    sequences = P(EVERY, None, None)
    rows = P(EVERY, None)
    vector = P(EVERY)
    in_specs = (
        (sequences, vector, P(), sequences)
        + (rows,) * 4
        + (vector,) * 2
        + (rows,) * 4
        + (vector,) * 2
    )
    out_specs = (sequences,) * 2 + (rows,) * 4 + (vector,) * 2 + (rows,) * 4 + (vector,) * 2
    return jax.shard_map(body, mesh=fine, in_specs=in_specs, out_specs=out_specs, check_vma=False)
```

```python
import math

import jax
import jax.numpy as jnp
from jax import lax
from jax.experimental import pallas as pl
from jax.experimental.pallas import tpu as pltpu
from jax.sharding import Mesh, PartitionSpec as P

HEADS = 8
KEY = 256
VAL = 512
EPSILON = 1e-05
RETAIN_EPSILON = 0.05
SCALE = KEY ** (-0.5)

EVERY = ("y", "x", "z", "core")
MEMBERS = ("y", "x", "core")
GROUP = 8
F32 = jnp.float32
BF16 = jnp.bfloat16


def dot(left, right):
    return jnp.dot(left, right, preferred_element_type=F32)


def dot_rows(left, right):
    return lax.dot_general(left, right, (((0,), (0,)), ((), ())), preferred_element_type=F32)


def dot_back(left, right):
    return lax.dot_general(left, right, (((1,), (1,)), ((), ())), preferred_element_type=F32)


def statistics(field_in, offset):
    centred = field_in - jnp.mean(field_in, axis=-1, keepdims=True)
    inverse = lax.rsqrt(jnp.mean(centred * centred, axis=-1, keepdims=True) + offset)
    return centred * inverse, inverse


def pull_back(hat, inverse, grad):
    return inverse * (
        grad
        - jnp.mean(grad, axis=-1, keepdims=True)
        - hat * jnp.mean(grad * hat, axis=-1, keepdims=True)
    )


def rotation_tables(length):
    half_width = KEY // 2
    columns = jnp.arange(half_width).astype(F32)
    angles = jnp.exp(-math.log(10000.0) * columns / (half_width - 1))
    zeta_scale = (2.0 * columns + 0.4 * KEY) / (1.4 * KEY)
    places = jnp.arange(length).astype(F32)[:, None]
    phases = places * angles[None, :]
    tables = []
    for direction in (1.0, -1.0):
        growth = jnp.exp(direction * places / 512.0 * jnp.log(zeta_scale)[None, :])
        tables += [jnp.cos(phases) * growth, jnp.sin(phases) * growth]
    return jnp.stack(tables)


def decay_mask(length, head):
    log_decay = jnp.log(1.0 - jnp.exp2(-5.0 - head.astype(F32)))
    places = jnp.arange(length)
    distance = (places[:, None] - places[None, :]).astype(F32)
    decayed = jnp.where(distance >= 0.0, jnp.exp(log_decay * jnp.maximum(distance, 0.0)), 0.0)
    return decayed * lax.rsqrt(jnp.sum(decayed, axis=-1, keepdims=True))


def read_rows(refs):
    return jnp.concatenate([ref[...] for ref in refs], axis=0) if len(refs) > 1 else refs[0][...]


def turn(field_in, cosine, sine):
    first, second = field_in[:, : KEY // 2], field_in[:, KEY // 2 :]
    return jnp.concatenate([first * cosine - second * sine, second * cosine + first * sine], axis=1)


def turn_back(field_in, cosine, sine):
    first, second = field_in[:, : KEY // 2], field_in[:, KEY // 2 :]
    return jnp.concatenate([first * cosine + second * sine, second * cosine - first * sine], axis=1)


def whole_spec(array):
    zeros = (0,) * array.ndim
    return pl.BlockSpec(array.shape, lambda i: zeros, pipeline_mode=pl.Buffered(1))


def pair_spec(shape, number):
    return pl.BlockSpec((2,) + shape, lambda i: (number,) + (0,) * len(shape))


def chunk_call(body_fn, name, number, pieces, shared, saved_in, buffers, shapes, parts, tokens=(), flops=0):
    flat = [piece for side in pieces for piece in side]
    counts = [len(side) for side in pieces]
    total = len(flat) + len(shared) + len(saved_in)
    carried = [] if buffers is None else list(buffers)

    def kernel(*refs):
        sides, at = [], 0
        for count in counts:
            sides.append(refs[at : at + count])
            at += count
        body_fn(sides, refs[at : at + len(shared)], refs[at + len(shared) : total], refs[total + len(carried) + len(tokens) :])

    outs = [jax.ShapeDtypeStruct((GROUP,) + shape, dtype) for shape, dtype in shapes]
    outs += [jax.ShapeDtypeStruct(shape, dtype) for shape, dtype in parts]
    operands = [*flat, *shared, *saved_in, *carried, *tokens]
    return pl.pallas_call(
        kernel,
        grid=(1,),
        out_shape=outs,
        in_specs=[whole_spec(o) for o in [*flat, *shared]]
        + [pair_spec(o.shape[1:], number) for o in saved_in]
        + [pl.BlockSpec(memory_space=pl.ANY) for _ in [*carried, *tokens]],
        out_specs=[pair_spec(shape, number) for shape, _ in shapes]
        + [pl.BlockSpec(shape, lambda i: (0, 0)) for shape, _ in parts],
        input_output_aliases={total + i: i for i in range(len(carried))},
        compiler_params=pltpu.CompilerParams(vmem_limit_bytes=56 * 1024 * 1024),
        cost_estimate=pl.CostEstimate(flops=flops, bytes_accessed=0, transcendentals=0),
        name=name,
    )(*operands)


def mixer_forward(sides, shared, saved_in, outs):
    features, tables, decay, weight, weight_o = shared
    normed_out, qkv_out, gate_out, gated_out = outs[:4]
    parts = outs[4:]
    cos_q, sin_q, cos_k, sin_k = (tables[i] for i in range(4))
    for s, side in enumerate(sides):
        hat, _ = statistics(read_rows(side).astype(F32), EPSILON)
        normed = (hat * features[0:1, :] + features[1:2, :]).astype(BF16)
        normed_out[s] = normed
        projected = dot(normed, weight[...])
        query_low = turn(projected[:, :KEY], cos_q, sin_q).astype(BF16)
        key_low = turn(projected[:, KEY : 2 * KEY], cos_k, sin_k).astype(BF16)
        value_low = projected[:, 2 * KEY : 2 * KEY + VAL].astype(BF16)
        gate = projected[:, 2 * KEY + VAL :]
        weighted = dot_back(query_low, key_low) * SCALE * decay[...]
        shaped = weighted * lax.rsqrt(1.0 + jnp.sum(weighted * weighted, axis=-1, keepdims=True))
        retained = dot(shaped.astype(BF16), value_low)
        retained_hat, _ = statistics(retained, RETAIN_EPSILON)
        qkv_out[s, :, :KEY] = query_low
        qkv_out[s, :, KEY : 2 * KEY] = key_low
        qkv_out[s, :, 2 * KEY :] = value_low
        gate_out[s] = gate
        gated = (gate * jax.nn.sigmoid(gate) * retained_hat).astype(BF16)
        gated_out[s] = gated
        parts[s][...] = dot(gated, weight_o[...]).astype(BF16)


def mixer_backward(sides, shared, saved_in, outs):
    tables, decay_ref, weight, weight_o = shared
    qkv, gate_ref = saved_in
    og_out, qk_out, vg_out = outs[:3]
    parts = outs[3:]
    cos_q, sin_q, cos_k, sin_k = (tables[i] for i in range(4))
    decay = decay_ref[...]
    for s, side in enumerate(sides):
        out_grad = read_rows(side)
        og_out[s] = out_grad
        gated_grad = dot_back(out_grad, weight_o[...])
        query_low = qkv[s, :, :KEY]
        key_low = qkv[s, :, KEY : 2 * KEY]
        value_low = qkv[s, :, 2 * KEY :]
        weighted = dot_back(query_low, key_low) * SCALE * decay
        inverse_c = lax.rsqrt(1.0 + jnp.sum(weighted * weighted, axis=-1, keepdims=True))
        shaped_low = (weighted * inverse_c).astype(BF16)
        retained_hat, inverse = statistics(dot(shaped_low, value_low), RETAIN_EPSILON)
        gate = gate_ref[s]
        sig = jax.nn.sigmoid(gate)
        gate_grad = (gated_grad * retained_hat * (sig * (1.0 + gate * (1.0 - sig)))).astype(BF16)
        retained_low = pull_back(retained_hat, inverse, gated_grad * (gate * sig)).astype(BF16)
        value_grad = dot_rows(shaped_low, retained_low).astype(BF16)
        shaped_grad = dot_back(retained_low, value_low)
        row_sum = jnp.sum(shaped_grad * weighted, axis=-1, keepdims=True)
        cubed = inverse_c * inverse_c * inverse_c
        score_grad = (decay * (shaped_grad * inverse_c - weighted * (row_sum * cubed))).astype(BF16)
        query_grad = turn_back(dot(score_grad, key_low) * SCALE, cos_q, sin_q).astype(BF16)
        key_grad = turn_back(dot_rows(score_grad, query_low) * SCALE, cos_k, sin_k).astype(BF16)
        both = jnp.concatenate([query_grad, key_grad], axis=1)
        value_gate = jnp.concatenate([value_grad, gate_grad], axis=1)
        qk_out[s] = both
        vg_out[s] = value_gate
        parts[s][...] = dot_back(jnp.concatenate([both, value_gate], axis=1), weight[...]).astype(BF16)


def feed_forward(sides, shared, saved_in, outs):
    (weight,) = shared
    normed_out, act_out, slopes_out, done = outs
    hidden = act_out.shape[2]
    done[...] = jnp.zeros_like(done)
    for s, side in enumerate(sides):
        normed = read_rows(side)
        normed_out[s] = normed
        pre = dot(normed, weight[...])
        gate_pre, up_pre = pre[:, :hidden], pre[:, hidden:]
        phi = 0.5 * (1.0 + lax.erf(gate_pre * math.sqrt(0.5)))
        gelu = gate_pre * phi
        slope = phi + gate_pre * (jnp.exp(-0.5 * gate_pre * gate_pre) * (1.0 / math.sqrt(2.0 * math.pi)))
        act_out[s] = (gelu * up_pre).astype(BF16)
        slopes_out[s, :, :hidden] = up_pre * slope
        slopes_out[s, :, hidden:] = gelu


def feed_backward(sides, shared, saved_in, outs):
    weight, down = shared
    act_ref, slopes, upstream_ref = saved_in
    pre_out = outs[0]
    feed_parts, normed_parts = outs[1:3], outs[3:5]
    for s in range(2):
        act_grad = dot_back(upstream_ref[s], down[...])
        low = (jnp.concatenate([act_grad, act_grad], axis=1) * slopes[s]).astype(BF16)
        pre_out[s] = low
        normed_parts[s][...] = dot_back(low, weight[...]).astype(BF16)
        feed_parts[s][...] = dot(act_ref[s], down[...]).astype(BF16)


def swap(field_in, axis):
    return lax.ppermute(field_in, axis, [(0, 1), (1, 0)])


def swap_both(field_in, axes):
    return lax.ppermute(field_in, axes, [(0, 3), (1, 2), (2, 1), (3, 0)])


def after(values, *tokens):
    anywhere = pl.BlockSpec(memory_space=pl.ANY)
    held = pl.pallas_call(
        lambda *refs: None,
        out_shape=[jax.ShapeDtypeStruct(v.shape, v.dtype) for v in values],
        in_specs=[anywhere] * (len(values) + len(tokens)),
        out_specs=[anywhere] * len(values),
        input_output_aliases={i: i for i in range(len(values))},
        cost_estimate=pl.CostEstimate(flops=0, bytes_accessed=0, transcendentals=0),
        name="after",
    )(*values, *tokens)
    return list(held)


def pair_up(pieces):
    return pieces, [swap(piece, "core") for piece in pieces]


def spread(own):
    half = own.shape[0] // 2
    from_x = swap(own, "x")
    from_y = swap(own, "y")
    upper = swap(from_y[:half], "x")
    lower = swap(from_x[half:], "y")
    return [pair_up(pieces) for pieces in ([own], [from_x], [from_y], [upper, lower])]


def chunks_in_turn(own, call):
    half = own.shape[0] // 2
    lower_x, upper_y = swap(own[half:], "x"), swap(own[:half], "y")
    chunk_own = pair_up([own])
    upper_x, lower_y = swap(own[:half], "x"), swap(own[half:], "y")
    results = [call(0, chunk_own, [])]
    lower_x, upper_y = after([lower_x, upper_y], results[0][-1])
    lower, upper = swap(lower_x, "y"), swap(upper_y, "x")
    upper_x, lower_y = after([upper_x, lower_y], lower_x)
    chunk_x, chunk_y = pair_up([upper_x, lower_x]), pair_up([upper_y, lower_y])
    results.append(call(1, chunk_x, results))
    chunk_across = pair_up(after([upper, lower], results[1][-1]))
    results.append(call(2, chunk_y, results))
    results.append(call(3, chunk_across, results))
    return results


def two_cores(pair):
    return pair[0].astype(F32) + swap(pair[1], "core").astype(F32)


class GroupSum:
    def __init__(self):
        self.passing = self.own = None
        self.arrived = []

    def terms(self, number, pair):
        total = two_cores(pair)
        half = total.shape[0] // 2
        if number == 0:
            self.own = total
            return None
        if number == 3:
            total = total.astype(BF16)
            self.passing = after([swap(total[half:], "y"), swap(total[:half], "x")])
            return total
        margins = ((half, 0), (0, half))[number - 1]
        passed = jnp.pad(self.passing[number - 1], (margins, (0, 0)))
        total = (total + passed.astype(F32)).astype(BF16)
        self.arrived.append(swap(total, ("x", "y")[number - 1]))
        return total

    def total(self, *tokens):
        arrived = after(self.arrived, *tokens) if tokens else self.arrived
        return self.own + arrived[0].astype(F32) + arrived[1].astype(F32)


def body(
    tokens,
    lengths,
    dealing,
    cotangent,
    query_weight,
    key_weight,
    value_weight,
    gate_weight,
    mixer_gain,
    mixer_bias,
    output_weight,
    feed_gate,
    feed_up,
    feed_down,
    feed_gain,
    feed_bias,
):
    _, length, breadth = tokens.shape
    layers = lax.axis_size("z")
    devices = 8 * layers
    local_model = query_weight.shape[0]
    local_hidden = feed_down.shape[0]
    local_value = output_weight.shape[0]
    hidden = local_hidden * layers
    half_layers = layers // 2
    fsdp_index = lax.axis_index("y") * 2 + lax.axis_index("x")
    core = lax.axis_index("core")
    layer = lax.axis_index("z")
    head = fsdp_index * 2 + core

    def to_members(packed, axes=MEMBERS):
        return lax.all_to_all(packed, axes, 0, 0, tiled=True)

    def gather_layers(mine):
        return lax.all_gather(
            mine.reshape(4, 2 * local_model, -1), "z", axis=1, tiled=True
        ).reshape(breadth, -1)

    def value_columns(weight):
        split = weight.reshape(local_model, 4, 2, half_layers, 2, local_value)
        return split.transpose(1, 2, 0, 4, 3, 5).reshape(GROUP, local_model, VAL)

    def head_columns(weight):
        return weight.reshape(local_model, HEADS, KEY).transpose(1, 0, 2)

    def hidden_columns(weight):
        split = weight.reshape(local_model, 4, layers, 2, local_hidden)
        return split.transpose(1, 3, 0, 2, 4).reshape(GROUP, local_model, hidden)

    weight_o = lax.all_gather(output_weight, "z", axis=0, tiled=True)
    mixer_mine = to_members(
        jnp.concatenate(
            [
                head_columns(query_weight),
                head_columns(key_weight),
                value_columns(value_weight),
                value_columns(gate_weight),
            ],
            axis=2,
        )
    )
    mixer_weight = gather_layers(mixer_mine)
    feed_packed = jnp.concatenate([hidden_columns(feed_gate), hidden_columns(feed_up)], axis=2)
    feed_mine = to_members(feed_packed)
    feed_weight = gather_layers(feed_mine)
    down_weight = lax.all_gather(feed_down, "z", axis=0, tiled=True)
    weight_o = to_members(weight_o, "core")

    vectors = jnp.stack([mixer_gain, mixer_bias, feed_gain, feed_bias])
    features = to_members(jnp.broadcast_to(vectors[None], (devices,) + vectors.shape), EVERY)
    features = features.transpose(1, 0, 2).reshape(4, breadth).astype(F32)

    slot_bits = []
    for bits_c in range(2):
        numbers = [
            ((fsdp_index ^ bits_f) * layers + layer) * 2 + (core ^ bits_c) for bits_f in range(4)
        ]
        slot_bits.append([fsdp_index ^ (dealing[n] // (2 * layers)) for n in numbers])
    sequence_in = []
    for slot in range(4):
        for bits_c in range(2):
            found = jnp.int32(0)
            for bits_f in range(1, 4):
                found = jnp.where(slot_bits[bits_c][bits_f] == slot, bits_f, found)
            sequence_in.append(found * 2 + bits_c)
    own_slot = slot_bits[0][0]

    places = jnp.arange(length, dtype=jnp.int32)
    live_mask = (places < lengths[0]).astype(F32)[:, None]
    upstream_own = (cotangent[0].astype(F32) * live_mask).astype(BF16)
    upstream_blocks = jnp.stack(
        [read for chunk in spread(upstream_own) for read in map(join, chunk)]
    )
    upstream_all = jnp.stack(
        [lax.dynamic_index_in_dim(upstream_blocks, n, 0, keepdims=False) for n in sequence_in]
    )

    tables = rotation_tables(length)
    decay = decay_mask(length, head)
    row_bytes = (length, breadth)
    saved, summed, leaving = None, GroupSum(), [upstream_all]
    token_chunks = spread(tokens[0])
    order = (3, 1, 2, 0)
    for i, n in enumerate(order):
        results = chunk_call(
            mixer_forward,
            "mixer_forward",
            n,
            token_chunks[n],
            [features[:2], tables, decay, mixer_weight, weight_o],
            [],
            saved,
            [
                ((length, breadth), BF16),
                ((length, 2 * KEY + VAL), BF16),
                ((length, VAL), F32),
                ((length, VAL), BF16),
            ],
            [(row_bytes, BF16)] * 2,
            leaving[: max(1, i)] if i < 3 else leaving,
        )
        saved = results[:4]
        leaving.append(summed.terms(n, results[4:6]))
    mixer_normed, qkv_all, gate_all, gated_all = saved
    hidden_state = tokens[0].astype(F32) + summed.total(feed_weight)

    feed_hat, feed_inverse = statistics(hidden_state, EPSILON)
    feed_own = (feed_hat * features[2] + features[3]).astype(BF16)

    def feed_call(n, chunk, earlier):
        return chunk_call(
            feed_forward,
            "feed_forward",
            n,
            chunk,
            [feed_weight],
            [],
            earlier[-1][:3] if earlier else None,
            [((length, breadth), BF16), ((length, hidden), BF16), ((length, 2 * hidden), F32)],
            [((8, 128), F32)],
            [down_weight] if n == 3 else [],
        )

    saved = chunks_in_turn(feed_own, feed_call)[-1][:3]
    feed_normed, activated, slopes = saved
    down_product = dot_rows(
        activated.reshape(GROUP * length, hidden), upstream_all.reshape(GROUP * length, breadth)
    ).astype(BF16)
    down_grad = lax.psum_scatter(down_product, "z", scatter_dimension=0, tiled=True)

    saved, summed, leaving, feed_parts = None, GroupSum(), [down_product], [None] * 4
    for i, n in enumerate(order):
        results = chunk_call(
            feed_backward,
            "feed_backward",
            n,
            [],
            [feed_weight, down_weight],
            [activated, slopes, upstream_all],
            saved,
            [((length, 2 * hidden), BF16)],
            [(row_bytes, BF16)] * 4,
            leaving[: max(1, i)] if i < 3 else leaving,
        )
        saved = results[:1]
        feed_parts[n] = results[1:3]
        leaving.append(summed.terms(n, results[3:5]))
    feed_product = dot_rows(
        feed_normed.reshape(GROUP * length, breadth),
        saved[0].reshape(GROUP * length, -1),
    ).astype(BF16)
    feed_normed_grad = summed.total(feed_product, down_grad)
    feed_gain_part = jnp.sum(feed_normed_grad * feed_hat, axis=0)
    feed_bias_part = jnp.sum(feed_normed_grad, axis=0)
    state_grad = upstream_all[0].astype(F32) + pull_back(
        feed_hat, feed_inverse, feed_normed_grad * features[2]
    )
    own_grad_low = state_grad.astype(BF16)

    def sum_layers(grads):
        return lax.psum_scatter(
            grads.reshape(4, -1, grads.shape[-1]), "z", scatter_dimension=1, tiled=True
        )

    def to_owners(mine):
        return to_members(mine.reshape(GROUP, local_model, -1))

    feed_summed = sum_layers(feed_product)
    feed_grads = to_owners(feed_summed)

    def backward_call(n, chunk, earlier):
        return chunk_call(
            mixer_backward,
            "mixer_backward",
            n,
            chunk,
            [tables, decay, mixer_weight, weight_o],
            [qkv_all, gate_all],
            earlier[-1][:3] if earlier else None,
            [((length, breadth), BF16), ((length, 2 * KEY), BF16), ((length, 2 * VAL), BF16)],
            [(row_bytes, BF16)] * 2,
            [],
            2 * 10**10,
        )

    results = chunks_in_turn(own_grad_low, backward_call)
    saved = results[-1][:3]
    out_grad, qk_grad, vg_grad = (a.reshape(GROUP * length, -1) for a in saved)
    (qk_grad,) = after([qk_grad], feed_summed)

    normed_rows = mixer_normed.reshape(GROUP * length, breadth)
    qk_product = dot_rows(normed_rows, qk_grad).astype(BF16)
    vg_product = dot_rows(normed_rows, vg_grad).astype(BF16)
    (out_grad,) = after([out_grad], feed_grads)
    out_product = dot_rows(gated_all.reshape(GROUP * length, VAL), out_grad).astype(BF16)
    qk_grads = to_owners(sum_layers(qk_product))
    vg_grads = to_owners(sum_layers(vg_product))
    output_grad = lax.psum_scatter(
        to_members(out_product, "core"), "z", scatter_dimension=0, tiled=True
    ).astype(F32)

    held = after([part for pair in feed_parts for part in pair], results[1][-1])
    summed = GroupSum()
    for n in order:
        summed.terms(n, held[2 * n : 2 * n + 2])
    slot_out = (hidden_state + summed.total(out_product)).astype(BF16)
    half = length // 2
    from_x, from_y = swap(slot_out, "x"), swap(slot_out, "y")
    across = jnp.concatenate([swap(from_y[:half], "x"), swap(from_x[half:], "y")], axis=0)
    (across,) = after([across], qk_grads)
    reached = jnp.stack([slot_out, from_x, from_y, across])
    chosen = lax.dynamic_index_in_dim(reached, own_slot, 0, keepdims=False)
    out_tokens = (live_mask * chosen.astype(F32)).astype(BF16)

    summed = GroupSum()
    for n in order:
        summed.terms(n, results[n][3:5])
    mixer_normed_grad = summed.total(out_product)
    mixer_hat, mixer_inverse = statistics(tokens[0].astype(F32), EPSILON)
    mixer_gain_part = jnp.sum(mixer_normed_grad * mixer_hat, axis=0)
    mixer_bias_part = jnp.sum(mixer_normed_grad, axis=0)
    input_grad = (
        state_grad + pull_back(mixer_hat, mixer_inverse, mixer_normed_grad * features[0])
    ).astype(BF16)

    def vector_grads(*grads):
        split = jnp.stack(grads).reshape(len(grads), devices, -1).transpose(1, 0, 2)
        return jnp.sum(to_members(split, EVERY), axis=0)

    feed_vectors = vector_grads(feed_gain_part, feed_bias_part)
    mixer_vectors = vector_grads(mixer_gain_part, mixer_bias_part)

    def head_back(grads):
        return grads.transpose(1, 0, 2).reshape(local_model, -1)

    def value_back(grads):
        split = grads.reshape(4, 2, local_model, 2, half_layers, local_value)
        return split.transpose(2, 0, 1, 4, 3, 5).reshape(local_model, -1)

    def hidden_back(grads):
        split = grads.reshape(4, 2, local_model, layers, local_hidden)
        return split.transpose(2, 0, 3, 1, 4).reshape(local_model, -1)

    return (
        out_tokens[None],
        input_grad[None],
        head_back(qk_grads[..., :KEY].astype(F32)),
        head_back(qk_grads[..., KEY:].astype(F32)),
        value_back(vg_grads[..., :VAL].astype(F32)),
        value_back(vg_grads[..., VAL:].astype(F32)),
        mixer_vectors[0],
        mixer_vectors[1],
        output_grad,
        hidden_back(feed_grads[..., :hidden].astype(F32)),
        hidden_back(feed_grads[..., hidden:].astype(F32)),
        down_grad.astype(F32),
        feed_vectors[0],
        feed_vectors[1],
    )


def join(pieces):
    return jnp.concatenate(pieces, axis=0) if len(pieces) > 1 else pieces[0]


def solution(mesh):
    layers = mesh.shape["dp"] // 2
    fine = Mesh(mesh.devices.reshape(2, 2, layers, 2), EVERY)
    sequences = P(EVERY, None, None)
    rows = P(EVERY, None)
    vector = P(EVERY)
    in_specs = (
        (sequences, vector, P(), sequences)
        + (rows,) * 4
        + (vector,) * 2
        + (rows,) * 4
        + (vector,) * 2
    )
    out_specs = (sequences,) * 2 + (rows,) * 4 + (vector,) * 2 + (rows,) * 4 + (vector,) * 2
    return jax.shard_map(body, mesh=fine, in_specs=in_specs, out_specs=out_specs, check_vma=False)
```

```python
import math

import jax
import jax.numpy as jnp
from jax import lax
from jax.experimental import pallas as pl
from jax.experimental.pallas import tpu as pltpu
from jax.sharding import Mesh, PartitionSpec as P

HEADS = 8
KEY = 256
VAL = 512
EPSILON = 1e-05
RETAIN_EPSILON = 0.05
SCALE = KEY ** (-0.5)

EVERY = ("y", "x", "z", "core")
MEMBERS = ("y", "x", "core")
GROUP = 8
F32 = jnp.float32
BF16 = jnp.bfloat16


def dot(left, right):
    return jnp.dot(left, right, preferred_element_type=F32)


def dot_rows(left, right):
    return lax.dot_general(left, right, (((0,), (0,)), ((), ())), preferred_element_type=F32)


def dot_back(left, right):
    return lax.dot_general(left, right, (((1,), (1,)), ((), ())), preferred_element_type=F32)


def statistics(field_in, offset):
    centred = field_in - jnp.mean(field_in, axis=-1, keepdims=True)
    inverse = lax.rsqrt(jnp.mean(centred * centred, axis=-1, keepdims=True) + offset)
    return centred * inverse, inverse


def pull_back(hat, inverse, grad):
    return inverse * (
        grad
        - jnp.mean(grad, axis=-1, keepdims=True)
        - hat * jnp.mean(grad * hat, axis=-1, keepdims=True)
    )


def rotation_tables(length):
    half_width = KEY // 2
    columns = jnp.arange(half_width).astype(F32)
    angles = jnp.exp(-math.log(10000.0) * columns / (half_width - 1))
    zeta_scale = (2.0 * columns + 0.4 * KEY) / (1.4 * KEY)
    places = jnp.arange(length).astype(F32)[:, None]
    phases = places * angles[None, :]
    tables = []
    for direction in (1.0, -1.0):
        growth = jnp.exp(direction * places / 512.0 * jnp.log(zeta_scale)[None, :])
        tables += [jnp.cos(phases) * growth, jnp.sin(phases) * growth]
    return jnp.stack(tables)


def decay_mask(length, head):
    log_decay = jnp.log(1.0 - jnp.exp2(-5.0 - head.astype(F32)))
    places = jnp.arange(length)
    distance = (places[:, None] - places[None, :]).astype(F32)
    decayed = jnp.where(distance >= 0.0, jnp.exp(log_decay * jnp.maximum(distance, 0.0)), 0.0)
    return decayed * lax.rsqrt(jnp.sum(decayed, axis=-1, keepdims=True))


def read_rows(refs):
    return jnp.concatenate([ref[...] for ref in refs], axis=0) if len(refs) > 1 else refs[0][...]


def turn(field_in, cosine, sine):
    first, second = field_in[:, : KEY // 2], field_in[:, KEY // 2 :]
    return jnp.concatenate([first * cosine - second * sine, second * cosine + first * sine], axis=1)


def turn_back(field_in, cosine, sine):
    first, second = field_in[:, : KEY // 2], field_in[:, KEY // 2 :]
    return jnp.concatenate([first * cosine + second * sine, second * cosine - first * sine], axis=1)


def whole_spec(array):
    zeros = (0,) * array.ndim
    return pl.BlockSpec(array.shape, lambda i: zeros, pipeline_mode=pl.Buffered(1))


def pair_spec(shape, number):
    return pl.BlockSpec((2,) + shape, lambda i: (number,) + (0,) * len(shape))


def chunk_call(body_fn, name, number, pieces, shared, saved_in, buffers, shapes, parts, tokens=(), flops=0):
    flat = [piece for side in pieces for piece in side]
    counts = [len(side) for side in pieces]
    total = len(flat) + len(shared) + len(saved_in)
    carried = [] if buffers is None else list(buffers)

    def kernel(*refs):
        sides, at = [], 0
        for count in counts:
            sides.append(refs[at : at + count])
            at += count
        body_fn(sides, refs[at : at + len(shared)], refs[at + len(shared) : total], refs[total + len(carried) + len(tokens) :])

    outs = [jax.ShapeDtypeStruct((GROUP,) + shape, dtype) for shape, dtype in shapes]
    outs += [jax.ShapeDtypeStruct(shape, dtype) for shape, dtype in parts]
    operands = [*flat, *shared, *saved_in, *carried, *tokens]
    return pl.pallas_call(
        kernel,
        grid=(1,),
        out_shape=outs,
        in_specs=[whole_spec(o) for o in [*flat, *shared]]
        + [pair_spec(o.shape[1:], number) for o in saved_in]
        + [pl.BlockSpec(memory_space=pl.ANY) for _ in [*carried, *tokens]],
        out_specs=[pair_spec(shape, number) for shape, _ in shapes]
        + [pl.BlockSpec(shape, lambda i: (0, 0)) for shape, _ in parts],
        input_output_aliases={total + i: i for i in range(len(carried))},
        compiler_params=pltpu.CompilerParams(vmem_limit_bytes=56 * 1024 * 1024),
        cost_estimate=pl.CostEstimate(flops=flops, bytes_accessed=0, transcendentals=0),
        name=name,
    )(*operands)


def mixer_forward(sides, shared, saved_in, outs):
    features, tables, decay, weight, weight_o = shared
    normed_out, qkv_out, gate_out, gated_out = outs[:4]
    parts = outs[4:]
    cos_q, sin_q, cos_k, sin_k = (tables[i] for i in range(4))
    for s, side in enumerate(sides):
        hat, _ = statistics(read_rows(side).astype(F32), EPSILON)
        normed = (hat * features[0:1, :] + features[1:2, :]).astype(BF16)
        normed_out[s] = normed
        projected = dot(normed, weight[...])
        query_low = turn(projected[:, :KEY], cos_q, sin_q).astype(BF16)
        key_low = turn(projected[:, KEY : 2 * KEY], cos_k, sin_k).astype(BF16)
        value_low = projected[:, 2 * KEY : 2 * KEY + VAL].astype(BF16)
        gate = projected[:, 2 * KEY + VAL :]
        weighted = dot_back(query_low, key_low) * SCALE * decay[...]
        shaped = weighted * lax.rsqrt(1.0 + jnp.sum(weighted * weighted, axis=-1, keepdims=True))
        retained = dot(shaped.astype(BF16), value_low)
        retained_hat, _ = statistics(retained, RETAIN_EPSILON)
        qkv_out[s, :, :KEY] = query_low
        qkv_out[s, :, KEY : 2 * KEY] = key_low
        qkv_out[s, :, 2 * KEY :] = value_low
        gate_out[s] = gate
        gated = (gate * jax.nn.sigmoid(gate) * retained_hat).astype(BF16)
        gated_out[s] = gated
        parts[s][...] = dot(gated, weight_o[...]).astype(BF16)


def mixer_backward(sides, shared, saved_in, outs):
    tables, decay_ref, weight, weight_o = shared
    qkv, gate_ref = saved_in
    og_out, qk_out, vg_out = outs[:3]
    parts = outs[3:]
    cos_q, sin_q, cos_k, sin_k = (tables[i] for i in range(4))
    decay = decay_ref[...]
    for s, side in enumerate(sides):
        out_grad = read_rows(side)
        og_out[s] = out_grad
        gated_grad = dot_back(out_grad, weight_o[...])
        query_low = qkv[s, :, :KEY]
        key_low = qkv[s, :, KEY : 2 * KEY]
        value_low = qkv[s, :, 2 * KEY :]
        weighted = dot_back(query_low, key_low) * SCALE * decay
        inverse_c = lax.rsqrt(1.0 + jnp.sum(weighted * weighted, axis=-1, keepdims=True))
        shaped_low = (weighted * inverse_c).astype(BF16)
        retained_hat, inverse = statistics(dot(shaped_low, value_low), RETAIN_EPSILON)
        gate = gate_ref[s]
        sig = jax.nn.sigmoid(gate)
        gate_grad = (gated_grad * retained_hat * (sig * (1.0 + gate * (1.0 - sig)))).astype(BF16)
        retained_low = pull_back(retained_hat, inverse, gated_grad * (gate * sig)).astype(BF16)
        value_grad = dot_rows(shaped_low, retained_low).astype(BF16)
        shaped_grad = dot_back(retained_low, value_low)
        row_sum = jnp.sum(shaped_grad * weighted, axis=-1, keepdims=True)
        cubed = inverse_c * inverse_c * inverse_c
        score_grad = (decay * (shaped_grad * inverse_c - weighted * (row_sum * cubed))).astype(BF16)
        query_grad = turn_back(dot(score_grad, key_low) * SCALE, cos_q, sin_q).astype(BF16)
        key_grad = turn_back(dot_rows(score_grad, query_low) * SCALE, cos_k, sin_k).astype(BF16)
        both = jnp.concatenate([query_grad, key_grad], axis=1)
        value_gate = jnp.concatenate([value_grad, gate_grad], axis=1)
        qk_out[s] = both
        vg_out[s] = value_gate
        parts[s][...] = dot_back(jnp.concatenate([both, value_gate], axis=1), weight[...]).astype(BF16)


def feed_forward(sides, shared, saved_in, outs):
    (weight,) = shared
    normed_out, act_out, slopes_out, done = outs
    hidden = act_out.shape[2]
    done[...] = jnp.zeros_like(done)
    for s, side in enumerate(sides):
        normed = read_rows(side)
        normed_out[s] = normed
        pre = dot(normed, weight[...])
        gate_pre, up_pre = pre[:, :hidden], pre[:, hidden:]
        phi = 0.5 * (1.0 + lax.erf(gate_pre * math.sqrt(0.5)))
        gelu = gate_pre * phi
        slope = phi + gate_pre * (jnp.exp(-0.5 * gate_pre * gate_pre) * (1.0 / math.sqrt(2.0 * math.pi)))
        act_out[s] = (gelu * up_pre).astype(BF16)
        slopes_out[s, :, :hidden] = up_pre * slope
        slopes_out[s, :, hidden:] = gelu


def feed_backward(sides, shared, saved_in, outs):
    weight, down = shared
    act_ref, slopes, upstream_ref = saved_in
    pre_out = outs[0]
    feed_parts, normed_parts = outs[1:3], outs[3:5]
    for s in range(2):
        act_grad = dot_back(upstream_ref[s], down[...])
        low = (jnp.concatenate([act_grad, act_grad], axis=1) * slopes[s]).astype(BF16)
        pre_out[s] = low
        normed_parts[s][...] = dot_back(low, weight[...]).astype(BF16)
        feed_parts[s][...] = dot(act_ref[s], down[...]).astype(BF16)


def lay_out(received, places):
    rows = received.shape[1]
    widths = [sum(place[3] for place in listed) for listed in places]
    if any(place[3] % 128 for listed in places for place in listed):
        return [
            jnp.concatenate(
                [received[m, :, a : a + w] for m, a, _, w in sorted(listed, key=lambda place: place[2])], axis=1
            ).astype(F32)
            for listed in places
        ]

    def kernel(block, *outs):
        for out, listed in zip(outs, places):
            for m, a, b, w in listed:
                out[:, b : b + w] = block[m, :, a : a + w].astype(F32)

    return pl.pallas_call(
        kernel,
        out_shape=[jax.ShapeDtypeStruct((rows, width), F32) for width in widths],
        name="lay_out",
    )(received)


def swap(field_in, axis):
    return lax.ppermute(field_in, axis, [(0, 1), (1, 0)])


def swap_both(field_in, axes):
    return lax.ppermute(field_in, axes, [(0, 3), (1, 2), (2, 1), (3, 0)])


def after(values, *tokens):
    anywhere = pl.BlockSpec(memory_space=pl.ANY)
    held = pl.pallas_call(
        lambda *refs: None,
        out_shape=[jax.ShapeDtypeStruct(v.shape, v.dtype) for v in values],
        in_specs=[anywhere] * (len(values) + len(tokens)),
        out_specs=[anywhere] * len(values),
        input_output_aliases={i: i for i in range(len(values))},
        cost_estimate=pl.CostEstimate(flops=0, bytes_accessed=0, transcendentals=0),
        name="after",
    )(*values, *tokens)
    return list(held)


def pair_up(pieces):
    return pieces, [swap(piece, "core") for piece in pieces]


def spread(own):
    half = own.shape[0] // 2
    from_x = swap(own, "x")
    from_y = swap(own, "y")
    upper = swap(from_y[:half], "x")
    lower = swap(from_x[half:], "y")
    return [pair_up(pieces) for pieces in ([own], [from_x], [from_y], [upper, lower])]


def chunks_in_turn(own, call):
    half = own.shape[0] // 2
    lower_x, upper_y = swap(own[half:], "x"), swap(own[:half], "y")
    chunk_own = pair_up([own])
    upper_x, lower_y = swap(own[:half], "x"), swap(own[half:], "y")
    results = [call(0, chunk_own, [])]
    lower_x, upper_y = after([lower_x, upper_y], results[0][-1])
    lower, upper = swap(lower_x, "y"), swap(upper_y, "x")
    upper_x, lower_y = after([upper_x, lower_y], lower_x)
    chunk_x, chunk_y = pair_up([upper_x, lower_x]), pair_up([upper_y, lower_y])
    results.append(call(1, chunk_x, results))
    chunk_across = pair_up(after([upper, lower], results[1][-1]))
    results.append(call(2, chunk_y, results))
    results.append(call(3, chunk_across, results))
    return results


def two_cores(pair):
    return pair[0].astype(F32) + swap(pair[1], "core").astype(F32)


class GroupSum:
    def __init__(self):
        self.passing = self.own = None
        self.arrived = []

    def terms(self, number, pair):
        total = two_cores(pair)
        half = total.shape[0] // 2
        if number == 0:
            self.own = total
            return None
        if number == 3:
            total = total.astype(BF16)
            self.passing = after([swap(total[half:], "y"), swap(total[:half], "x")])
            return total
        margins = ((half, 0), (0, half))[number - 1]
        passed = jnp.pad(self.passing[number - 1], (margins, (0, 0)))
        total = (total + passed.astype(F32)).astype(BF16)
        self.arrived.append(swap(total, ("x", "y")[number - 1]))
        return total

    def total(self, *tokens):
        arrived = after(self.arrived, *tokens) if tokens else self.arrived
        return self.own + arrived[0].astype(F32) + arrived[1].astype(F32)


def body(
    tokens,
    lengths,
    dealing,
    cotangent,
    query_weight,
    key_weight,
    value_weight,
    gate_weight,
    mixer_gain,
    mixer_bias,
    output_weight,
    feed_gate,
    feed_up,
    feed_down,
    feed_gain,
    feed_bias,
):
    _, length, breadth = tokens.shape
    layers = lax.axis_size("z")
    devices = 8 * layers
    local_model = query_weight.shape[0]
    local_hidden = feed_down.shape[0]
    local_value = output_weight.shape[0]
    hidden = local_hidden * layers
    half_layers = layers // 2
    fsdp_index = lax.axis_index("y") * 2 + lax.axis_index("x")
    core = lax.axis_index("core")
    layer = lax.axis_index("z")
    head = fsdp_index * 2 + core

    def to_members(packed, axes=MEMBERS):
        return lax.all_to_all(packed, axes, 0, 0, tiled=True)

    def gather_layers(mine):
        return lax.all_gather(
            mine.reshape(4, 2 * local_model, -1), "z", axis=1, tiled=True
        ).reshape(breadth, -1)

    def value_columns(weight):
        split = weight.reshape(local_model, 4, 2, half_layers, 2, local_value)
        return split.transpose(1, 2, 0, 4, 3, 5).reshape(GROUP, local_model, VAL)

    def head_columns(weight):
        return weight.reshape(local_model, HEADS, KEY).transpose(1, 0, 2)

    def hidden_columns(weight):
        split = weight.reshape(local_model, 4, layers, 2, local_hidden)
        return split.transpose(1, 3, 0, 2, 4).reshape(GROUP, local_model, hidden)

    weight_o = lax.all_gather(output_weight, "z", axis=0, tiled=True)
    mixer_mine = to_members(
        jnp.concatenate(
            [
                head_columns(query_weight),
                head_columns(key_weight),
                value_columns(value_weight),
                value_columns(gate_weight),
            ],
            axis=2,
        )
    )
    mixer_weight = gather_layers(mixer_mine)
    feed_packed = jnp.concatenate([hidden_columns(feed_gate), hidden_columns(feed_up)], axis=2)
    feed_mine = to_members(feed_packed)
    feed_weight = gather_layers(feed_mine)
    down_weight = lax.all_gather(feed_down, "z", axis=0, tiled=True)
    weight_o = to_members(weight_o, "core")

    vectors = jnp.stack([mixer_gain, mixer_bias, feed_gain, feed_bias])
    features = to_members(jnp.broadcast_to(vectors[None], (devices,) + vectors.shape), EVERY)
    features = features.transpose(1, 0, 2).reshape(4, breadth).astype(F32)

    slot_bits = []
    for bits_c in range(2):
        numbers = [
            ((fsdp_index ^ bits_f) * layers + layer) * 2 + (core ^ bits_c) for bits_f in range(4)
        ]
        slot_bits.append([fsdp_index ^ (dealing[n] // (2 * layers)) for n in numbers])
    sequence_in = []
    for slot in range(4):
        for bits_c in range(2):
            found = jnp.int32(0)
            for bits_f in range(1, 4):
                found = jnp.where(slot_bits[bits_c][bits_f] == slot, bits_f, found)
            sequence_in.append(found * 2 + bits_c)
    own_slot = slot_bits[0][0]

    places = jnp.arange(length, dtype=jnp.int32)
    live_mask = (places < lengths[0]).astype(F32)[:, None]
    upstream_own = (cotangent[0].astype(F32) * live_mask).astype(BF16)
    upstream_blocks = jnp.stack(
        [read for chunk in spread(upstream_own) for read in map(join, chunk)]
    )
    upstream_all = jnp.stack(
        [lax.dynamic_index_in_dim(upstream_blocks, n, 0, keepdims=False) for n in sequence_in]
    )

    tables = rotation_tables(length)
    decay = decay_mask(length, head)
    row_bytes = (length, breadth)
    saved, summed, leaving = None, GroupSum(), [upstream_all]
    token_chunks = spread(tokens[0])
    order = (3, 1, 2, 0)
    for i, n in enumerate(order):
        results = chunk_call(
            mixer_forward,
            "mixer_forward",
            n,
            token_chunks[n],
            [features[:2], tables, decay, mixer_weight, weight_o],
            [],
            saved,
            [
                ((length, breadth), BF16),
                ((length, 2 * KEY + VAL), BF16),
                ((length, VAL), F32),
                ((length, VAL), BF16),
            ],
            [(row_bytes, BF16)] * 2,
            leaving[: max(1, i)] if i < 3 else leaving,
        )
        saved = results[:4]
        leaving.append(summed.terms(n, results[4:6]))
    mixer_normed, qkv_all, gate_all, gated_all = saved
    hidden_state = tokens[0].astype(F32) + summed.total(feed_weight)

    feed_hat, feed_inverse = statistics(hidden_state, EPSILON)
    feed_own = (feed_hat * features[2] + features[3]).astype(BF16)

    def feed_call(n, chunk, earlier):
        return chunk_call(
            feed_forward,
            "feed_forward",
            n,
            chunk,
            [feed_weight],
            [],
            earlier[-1][:3] if earlier else None,
            [((length, breadth), BF16), ((length, hidden), BF16), ((length, 2 * hidden), F32)],
            [((8, 128), F32)],
            [down_weight] if n == 3 else [],
        )

    saved = chunks_in_turn(feed_own, feed_call)[-1][:3]
    feed_normed, activated, slopes = saved
    down_product = dot_rows(
        activated.reshape(GROUP * length, hidden), upstream_all.reshape(GROUP * length, breadth)
    ).astype(BF16)
    down_grad = lax.psum_scatter(down_product, "z", scatter_dimension=0, tiled=True)

    saved, summed, leaving, feed_parts = None, GroupSum(), [down_product], [None] * 4
    for i, n in enumerate(order):
        results = chunk_call(
            feed_backward,
            "feed_backward",
            n,
            [],
            [feed_weight, down_weight],
            [activated, slopes, upstream_all],
            saved,
            [((length, 2 * hidden), BF16)],
            [(row_bytes, BF16)] * 4,
            leaving[: max(1, i)] if i < 3 else leaving,
        )
        saved = results[:1]
        feed_parts[n] = results[1:3]
        leaving.append(summed.terms(n, results[3:5]))
    feed_product = dot_rows(
        feed_normed.reshape(GROUP * length, breadth),
        saved[0].reshape(GROUP * length, -1),
    ).astype(BF16)
    feed_normed_grad = summed.total(feed_product, down_grad)
    feed_gain_part = jnp.sum(feed_normed_grad * feed_hat, axis=0)
    feed_bias_part = jnp.sum(feed_normed_grad, axis=0)
    state_grad = upstream_all[0].astype(F32) + pull_back(
        feed_hat, feed_inverse, feed_normed_grad * features[2]
    )
    own_grad_low = state_grad.astype(BF16)

    def sum_layers(grads):
        return lax.psum_scatter(
            grads.reshape(4, -1, grads.shape[-1]), "z", scatter_dimension=1, tiled=True
        )

    def to_owners(mine):
        return to_members(mine.reshape(GROUP, local_model, -1))

    feed_summed = sum_layers(feed_product)
    feed_grads = to_owners(feed_summed)

    feed_terms, held, leaving = GroupSum(), [], []

    def backward_call(n, chunk, earlier):
        if n == 3:
            held.extend(after([part for pair in feed_parts for part in pair], earlier[1][-1]))
            leaving.append(feed_terms.terms(3, held[6:]))
        return chunk_call(
            mixer_backward,
            "mixer_backward",
            n,
            chunk,
            [tables, decay, mixer_weight, weight_o],
            [qkv_all, gate_all],
            earlier[-1][:3] if earlier else None,
            [((length, breadth), BF16), ((length, 2 * KEY), BF16), ((length, 2 * VAL), BF16)],
            [(row_bytes, BF16)] * 2,
            leaving,
            2 * 10**10,
        )

    results = chunks_in_turn(own_grad_low, backward_call)
    saved = results[-1][:3]
    out_grad, qk_grad, vg_grad = (a.reshape(GROUP * length, -1) for a in saved)
    (qk_grad,) = after([qk_grad], feed_summed)
    leaving = [feed_terms.terms(number, held[2 * number :][:2]) for number in (1, 2)]
    (vg_grad,) = after([vg_grad], *leaving)
    feed_terms.terms(0, held[:2])

    normed_rows = mixer_normed.reshape(GROUP * length, breadth)
    qk_product = dot_rows(normed_rows, qk_grad).astype(BF16)
    vg_product = dot_rows(normed_rows, vg_grad).astype(BF16)
    qk_grads = to_owners(sum_layers(qk_product))
    (out_grad,) = after([out_grad], feed_grads, qk_grads)
    out_product = dot_rows(gated_all.reshape(GROUP * length, VAL), out_grad).astype(BF16)
    vg_grads = to_owners(sum_layers(vg_product))
    output_grad = lax.psum_scatter(
        to_members(out_product, "core"), "z", scatter_dimension=0, tiled=True
    ).astype(F32)

    slot_out = (hidden_state + feed_terms.total()).astype(BF16)
    half = length // 2
    from_x, from_y = swap(slot_out, "x"), swap(slot_out, "y")
    across = jnp.concatenate(
        after([swap(from_y[:half], "x"), swap(from_x[half:], "y")], vg_grads), axis=0
    )
    reached = jnp.stack([slot_out, from_x, from_y, across])
    chosen = lax.dynamic_index_in_dim(reached, own_slot, 0, keepdims=False)
    out_tokens = (live_mask * chosen.astype(F32)).astype(BF16)

    summed = GroupSum()
    for n in order:
        summed.terms(n, results[n][3:5])
    mixer_normed_grad = summed.total(out_product, vg_grads)
    mixer_hat, mixer_inverse = statistics(tokens[0].astype(F32), EPSILON)
    mixer_gain_part = jnp.sum(mixer_normed_grad * mixer_hat, axis=0)
    mixer_bias_part = jnp.sum(mixer_normed_grad, axis=0)
    input_grad = (
        state_grad + pull_back(mixer_hat, mixer_inverse, mixer_normed_grad * features[0])
    ).astype(BF16)

    def vector_grads(*grads):
        split = jnp.stack(grads).reshape(len(grads), devices, -1).transpose(1, 0, 2)
        return jnp.sum(to_members(split, EVERY), axis=0)

    vector_sums = vector_grads(mixer_gain_part, mixer_bias_part, feed_gain_part, feed_bias_part)

    def head_places(at):
        return [(member, at, member * KEY, KEY) for member in range(GROUP)]

    def value_places(at):
        return [
            (member, at + (c * half_layers + l) * local_value, ((member * half_layers + l) * 2 + c) * local_value, local_value)
            for member in range(GROUP)
            for l in range(half_layers)
            for c in range(2)
        ]

    def hidden_places(at):
        return [
            (f * 2 + c, at + l * local_hidden, ((f * layers + l) * 2 + c) * local_hidden, local_hidden)
            for f in range(4)
            for l in range(layers)
            for c in range(2)
        ]

    query_grad, key_grad = lay_out(qk_grads, [head_places(0), head_places(KEY)])
    value_grad, gate_grad = lay_out(vg_grads, [value_places(0), value_places(VAL)])
    feed_gate_grad, feed_up_grad = lay_out(feed_grads, [hidden_places(0), hidden_places(hidden)])

    return (
        out_tokens[None],
        input_grad[None],
        query_grad,
        key_grad,
        value_grad,
        gate_grad,
        vector_sums[0],
        vector_sums[1],
        output_grad,
        feed_gate_grad,
        feed_up_grad,
        down_grad.astype(F32),
        vector_sums[2],
        vector_sums[3],
    )


def join(pieces):
    return jnp.concatenate(pieces, axis=0) if len(pieces) > 1 else pieces[0]


def solution(mesh):
    layers = mesh.shape["dp"] // 2
    fine = Mesh(mesh.devices.reshape(2, 2, layers, 2), EVERY)
    sequences = P(EVERY, None, None)
    rows = P(EVERY, None)
    vector = P(EVERY)
    in_specs = (
        (sequences, vector, P(), sequences)
        + (rows,) * 4
        + (vector,) * 2
        + (rows,) * 4
        + (vector,) * 2
    )
    out_specs = (sequences,) * 2 + (rows,) * 4 + (vector,) * 2 + (rows,) * 4 + (vector,) * 2
    return jax.shard_map(body, mesh=fine, in_specs=in_specs, out_specs=out_specs, check_vma=False)
```

```python
import math

import jax
import jax.numpy as jnp
from jax import lax
from jax.experimental import pallas as pl
from jax.experimental.pallas import tpu as pltpu
from jax.sharding import Mesh, PartitionSpec as P

HEADS = 8
KEY = 256
VAL = 512
EPSILON = 1e-05
RETAIN_EPSILON = 0.05
SCALE = KEY ** (-0.5)

EVERY = ("y", "x", "z", "core")
MEMBERS = ("y", "x", "core")
GROUP = 8
F32 = jnp.float32
BF16 = jnp.bfloat16


def dot(left, right):
    return jnp.dot(left, right, preferred_element_type=F32)


def dot_rows(left, right):
    return lax.dot_general(left, right, (((0,), (0,)), ((), ())), preferred_element_type=F32)


def dot_back(left, right):
    return lax.dot_general(left, right, (((1,), (1,)), ((), ())), preferred_element_type=F32)


def statistics(field_in, offset):
    centred = field_in - jnp.mean(field_in, axis=-1, keepdims=True)
    inverse = lax.rsqrt(jnp.mean(centred * centred, axis=-1, keepdims=True) + offset)
    return centred * inverse, inverse


def pull_back(hat, inverse, grad):
    return inverse * (
        grad
        - jnp.mean(grad, axis=-1, keepdims=True)
        - hat * jnp.mean(grad * hat, axis=-1, keepdims=True)
    )


def rotation_tables(length):
    half_width = KEY // 2
    columns = jnp.arange(half_width).astype(F32)
    angles = jnp.exp(-math.log(10000.0) * columns / (half_width - 1))
    zeta_scale = (2.0 * columns + 0.4 * KEY) / (1.4 * KEY)
    places = jnp.arange(length).astype(F32)[:, None]
    phases = places * angles[None, :]
    tables = []
    for direction in (1.0, -1.0):
        growth = jnp.exp(direction * places / 512.0 * jnp.log(zeta_scale)[None, :])
        tables += [jnp.cos(phases) * growth, jnp.sin(phases) * growth]
    return jnp.stack(tables)


def decay_mask(length, head):
    log_decay = jnp.log(1.0 - jnp.exp2(-5.0 - head.astype(F32)))
    places = jnp.arange(length)
    distance = (places[:, None] - places[None, :]).astype(F32)
    decayed = jnp.where(distance >= 0.0, jnp.exp(log_decay * jnp.maximum(distance, 0.0)), 0.0)
    return decayed * lax.rsqrt(jnp.sum(decayed, axis=-1, keepdims=True))


def read_rows(refs):
    return jnp.concatenate([ref[...] for ref in refs], axis=0) if len(refs) > 1 else refs[0][...]


def turn(field_in, cosine, sine):
    first, second = field_in[:, : KEY // 2], field_in[:, KEY // 2 :]
    return jnp.concatenate([first * cosine - second * sine, second * cosine + first * sine], axis=1)


def turn_back(field_in, cosine, sine):
    first, second = field_in[:, : KEY // 2], field_in[:, KEY // 2 :]
    return jnp.concatenate([first * cosine + second * sine, second * cosine - first * sine], axis=1)


def whole_spec(array):
    zeros = (0,) * array.ndim
    return pl.BlockSpec(array.shape, lambda i: zeros, pipeline_mode=pl.Buffered(1))


def pair_spec(shape, number):
    return pl.BlockSpec((2,) + shape, lambda i: (number,) + (0,) * len(shape))


def chunk_call(body_fn, name, number, pieces, shared, saved_in, buffers, shapes, parts, tokens=(), flops=0):
    flat = [piece for side in pieces for piece in side]
    counts = [len(side) for side in pieces]
    total = len(flat) + len(shared) + len(saved_in)
    carried = [] if buffers is None else list(buffers)

    def kernel(*refs):
        sides, at = [], 0
        for count in counts:
            sides.append(refs[at : at + count])
            at += count
        body_fn(sides, refs[at : at + len(shared)], refs[at + len(shared) : total], refs[total + len(carried) + len(tokens) :])

    outs = [jax.ShapeDtypeStruct((GROUP,) + shape, dtype) for shape, dtype in shapes]
    outs += [jax.ShapeDtypeStruct(shape, dtype) for shape, dtype in parts]
    operands = [*flat, *shared, *saved_in, *carried, *tokens]
    return pl.pallas_call(
        kernel,
        grid=(1,),
        out_shape=outs,
        in_specs=[whole_spec(o) for o in [*flat, *shared]]
        + [pair_spec(o.shape[1:], number) for o in saved_in]
        + [pl.BlockSpec(memory_space=pl.ANY) for _ in [*carried, *tokens]],
        out_specs=[pair_spec(shape, number) for shape, _ in shapes]
        + [pl.BlockSpec(shape, lambda i: (0, 0)) for shape, _ in parts],
        input_output_aliases={total + i: i for i in range(len(carried))},
        compiler_params=pltpu.CompilerParams(vmem_limit_bytes=56 * 1024 * 1024),
        cost_estimate=pl.CostEstimate(flops=flops, bytes_accessed=0, transcendentals=0),
        name=name,
    )(*operands)


def mixer_forward(sides, shared, saved_in, outs):
    features, tables, decay, weight, weight_o = shared
    normed_out, qkv_out, gate_out, gated_out = outs[:4]
    parts = outs[4:]
    cos_q, sin_q, cos_k, sin_k = (tables[i] for i in range(4))
    for s, side in enumerate(sides):
        hat, _ = statistics(read_rows(side).astype(F32), EPSILON)
        normed = (hat * features[0:1, :] + features[1:2, :]).astype(BF16)
        normed_out[s] = normed
        projected = dot(normed, weight[...])
        query_low = turn(projected[:, :KEY], cos_q, sin_q).astype(BF16)
        key_low = turn(projected[:, KEY : 2 * KEY], cos_k, sin_k).astype(BF16)
        value_low = projected[:, 2 * KEY : 2 * KEY + VAL].astype(BF16)
        gate = projected[:, 2 * KEY + VAL :]
        weighted = dot_back(query_low, key_low) * SCALE * decay[...]
        shaped = weighted * lax.rsqrt(1.0 + jnp.sum(weighted * weighted, axis=-1, keepdims=True))
        retained = dot(shaped.astype(BF16), value_low)
        retained_hat, _ = statistics(retained, RETAIN_EPSILON)
        qkv_out[s, :, :KEY] = query_low
        qkv_out[s, :, KEY : 2 * KEY] = key_low
        qkv_out[s, :, 2 * KEY :] = value_low
        gate_out[s] = gate
        gated = (gate * jax.nn.sigmoid(gate) * retained_hat).astype(BF16)
        gated_out[s] = gated
        parts[s][...] = dot(gated, weight_o[...]).astype(BF16)


def mixer_backward(sides, shared, saved_in, outs):
    tables, decay_ref, weight, weight_o = shared
    qkv, gate_ref = saved_in
    og_out, qk_out, vg_out = outs[:3]
    parts = outs[3:]
    cos_q, sin_q, cos_k, sin_k = (tables[i] for i in range(4))
    decay = decay_ref[...]
    for s, side in enumerate(sides):
        out_grad = read_rows(side)
        og_out[s] = out_grad
        gated_grad = dot_back(out_grad, weight_o[...])
        query_low = qkv[s, :, :KEY]
        key_low = qkv[s, :, KEY : 2 * KEY]
        value_low = qkv[s, :, 2 * KEY :]
        weighted = dot_back(query_low, key_low) * SCALE * decay
        inverse_c = lax.rsqrt(1.0 + jnp.sum(weighted * weighted, axis=-1, keepdims=True))
        shaped_low = (weighted * inverse_c).astype(BF16)
        retained_hat, inverse = statistics(dot(shaped_low, value_low), RETAIN_EPSILON)
        gate = gate_ref[s]
        sig = jax.nn.sigmoid(gate)
        gate_grad = (gated_grad * retained_hat * (sig * (1.0 + gate * (1.0 - sig)))).astype(BF16)
        retained_low = pull_back(retained_hat, inverse, gated_grad * (gate * sig)).astype(BF16)
        value_grad = dot_rows(shaped_low, retained_low).astype(BF16)
        shaped_grad = dot_back(retained_low, value_low)
        row_sum = jnp.sum(shaped_grad * weighted, axis=-1, keepdims=True)
        cubed = inverse_c * inverse_c * inverse_c
        score_grad = (decay * (shaped_grad * inverse_c - weighted * (row_sum * cubed))).astype(BF16)
        query_grad = turn_back(dot(score_grad, key_low) * SCALE, cos_q, sin_q).astype(BF16)
        key_grad = turn_back(dot_rows(score_grad, query_low) * SCALE, cos_k, sin_k).astype(BF16)
        both = jnp.concatenate([query_grad, key_grad], axis=1)
        value_gate = jnp.concatenate([value_grad, gate_grad], axis=1)
        qk_out[s] = both
        vg_out[s] = value_gate
        parts[s][...] = dot_back(jnp.concatenate([both, value_gate], axis=1), weight[...]).astype(BF16)


def feed_forward(sides, shared, saved_in, outs):
    (weight,) = shared
    normed_out, act_out, slopes_out, done = outs
    hidden = act_out.shape[2]
    done[...] = jnp.zeros_like(done)
    for s, side in enumerate(sides):
        normed = read_rows(side)
        normed_out[s] = normed
        pre = dot(normed, weight[...])
        gate_pre, up_pre = pre[:, :hidden], pre[:, hidden:]
        phi = 0.5 * (1.0 + lax.erf(gate_pre * math.sqrt(0.5)))
        gelu = gate_pre * phi
        slope = phi + gate_pre * (jnp.exp(-0.5 * gate_pre * gate_pre) * (1.0 / math.sqrt(2.0 * math.pi)))
        act_out[s] = (gelu * up_pre).astype(BF16)
        slopes_out[s, :, :hidden] = up_pre * slope
        slopes_out[s, :, hidden:] = gelu


def feed_backward(sides, shared, saved_in, outs):
    weight, down = shared
    act_ref, slopes, upstream_ref = saved_in
    pre_out = outs[0]
    feed_parts, normed_parts = outs[1:3], outs[3:5]
    for s in range(2):
        act_grad = dot_back(upstream_ref[s], down[...])
        low = (jnp.concatenate([act_grad, act_grad], axis=1) * slopes[s]).astype(BF16)
        pre_out[s] = low
        normed_parts[s][...] = dot_back(low, weight[...]).astype(BF16)
        feed_parts[s][...] = dot(act_ref[s], down[...]).astype(BF16)


def lay_out(received, places):
    rows = received.shape[1]
    widths = [sum(place[3] for place in listed) for listed in places]
    if any(place[3] % 128 for listed in places for place in listed):
        return [
            jnp.concatenate(
                [received[m, :, a : a + w] for m, a, _, w in sorted(listed, key=lambda place: place[2])], axis=1
            ).astype(F32)
            for listed in places
        ]

    def kernel(block, *outs):
        for out, listed in zip(outs, places):
            for m, a, b, w in listed:
                out[:, b : b + w] = block[m, :, a : a + w].astype(F32)

    return pl.pallas_call(
        kernel,
        out_shape=[jax.ShapeDtypeStruct((rows, width), F32) for width in widths],
        name="lay_out",
    )(received)


def swap(field_in, axis):
    return lax.ppermute(field_in, axis, [(0, 1), (1, 0)])


def swap_both(field_in, axes):
    return lax.ppermute(field_in, axes, [(0, 3), (1, 2), (2, 1), (3, 0)])


def after(values, *tokens):
    anywhere = pl.BlockSpec(memory_space=pl.ANY)
    held = pl.pallas_call(
        lambda *refs: None,
        out_shape=[jax.ShapeDtypeStruct(v.shape, v.dtype) for v in values],
        in_specs=[anywhere] * (len(values) + len(tokens)),
        out_specs=[anywhere] * len(values),
        input_output_aliases={i: i for i in range(len(values))},
        cost_estimate=pl.CostEstimate(flops=0, bytes_accessed=0, transcendentals=0),
        name="after",
    )(*values, *tokens)
    return list(held)


def pair_up(pieces):
    return pieces, [swap(piece, "core") for piece in pieces]


def spread(own):
    half = own.shape[0] // 2
    from_x = swap(own, "x")
    from_y = swap(own, "y")
    upper = swap(from_y[:half], "x")
    lower = swap(from_x[half:], "y")
    return [pair_up(pieces) for pieces in ([own], [from_x], [from_y], [upper, lower])]


def chunks_in_turn(own, call):
    half = own.shape[0] // 2
    lower_x, upper_y = swap(own[half:], "x"), swap(own[:half], "y")
    chunk_own = pair_up([own])
    upper_x, lower_y = swap(own[:half], "x"), swap(own[half:], "y")
    results = [call(0, chunk_own, [])]
    lower_x, upper_y = after([lower_x, upper_y], results[0][-1])
    lower, upper = swap(lower_x, "y"), swap(upper_y, "x")
    upper_x, lower_y = after([upper_x, lower_y], lower_x)
    chunk_x, chunk_y = pair_up([upper_x, lower_x]), pair_up([upper_y, lower_y])
    results.append(call(1, chunk_x, results))
    chunk_across = pair_up(after([upper, lower], results[1][-1]))
    results.append(call(2, chunk_y, results))
    results.append(call(3, chunk_across, results))
    return results


def two_cores(pair):
    return pair[0].astype(F32) + swap(pair[1], "core").astype(F32)


class GroupSum:
    def __init__(self):
        self.passing = self.own = None
        self.arrived = []

    def terms(self, number, pair):
        total = two_cores(pair)
        half = total.shape[0] // 2
        if number == 0:
            self.own = total
            return None
        if number == 3:
            total = total.astype(BF16)
            self.passing = after([swap(total[half:], "y"), swap(total[:half], "x")])
            return total
        margins = ((half, 0), (0, half))[number - 1]
        passed = jnp.pad(self.passing[number - 1], (margins, (0, 0)))
        total = (total + passed.astype(F32)).astype(BF16)
        self.arrived.append(swap(total, ("x", "y")[number - 1]))
        return total

    def total(self, *tokens):
        arrived = after(self.arrived, *tokens) if tokens else self.arrived
        return self.own + arrived[0].astype(F32) + arrived[1].astype(F32)


def body(
    tokens,
    lengths,
    dealing,
    cotangent,
    query_weight,
    key_weight,
    value_weight,
    gate_weight,
    mixer_gain,
    mixer_bias,
    output_weight,
    feed_gate,
    feed_up,
    feed_down,
    feed_gain,
    feed_bias,
):
    _, length, breadth = tokens.shape
    layers = lax.axis_size("z")
    devices = 8 * layers
    local_model = query_weight.shape[0]
    local_hidden = feed_down.shape[0]
    local_value = output_weight.shape[0]
    hidden = local_hidden * layers
    half_layers = layers // 2
    fsdp_index = lax.axis_index("y") * 2 + lax.axis_index("x")
    core = lax.axis_index("core")
    layer = lax.axis_index("z")
    head = fsdp_index * 2 + core

    def to_members(packed, axes=MEMBERS):
        return lax.all_to_all(packed, axes, 0, 0, tiled=True)

    def gather_layers(mine):
        return lax.all_gather(
            mine.reshape(4, 2 * local_model, -1), "z", axis=1, tiled=True
        ).reshape(breadth, -1)

    def value_columns(weight):
        split = weight.reshape(local_model, 4, 2, half_layers, 2, local_value)
        return split.transpose(1, 2, 0, 4, 3, 5).reshape(GROUP, local_model, VAL)

    def head_columns(weight):
        return weight.reshape(local_model, HEADS, KEY).transpose(1, 0, 2)

    def hidden_columns(weight):
        split = weight.reshape(local_model, 4, layers, 2, local_hidden)
        return split.transpose(1, 3, 0, 2, 4).reshape(GROUP, local_model, hidden)

    weight_o = lax.all_gather(output_weight, "z", axis=0, tiled=True)
    mixer_mine = to_members(
        jnp.concatenate(
            [
                head_columns(query_weight),
                head_columns(key_weight),
                value_columns(value_weight),
                value_columns(gate_weight),
            ],
            axis=2,
        )
    )
    mixer_weight = gather_layers(mixer_mine)
    feed_packed = jnp.concatenate([hidden_columns(feed_gate), hidden_columns(feed_up)], axis=2)
    feed_mine = to_members(feed_packed)
    feed_weight = gather_layers(feed_mine)
    down_weight = lax.all_gather(feed_down, "z", axis=0, tiled=True)
    weight_o = to_members(weight_o, "core")

    vectors = jnp.stack([mixer_gain, mixer_bias, feed_gain, feed_bias])
    features = to_members(jnp.broadcast_to(vectors[None], (devices,) + vectors.shape), EVERY)
    features = features.transpose(1, 0, 2).reshape(4, breadth).astype(F32)

    slot_bits = []
    for bits_c in range(2):
        numbers = [
            ((fsdp_index ^ bits_f) * layers + layer) * 2 + (core ^ bits_c) for bits_f in range(4)
        ]
        slot_bits.append([fsdp_index ^ (dealing[n] // (2 * layers)) for n in numbers])
    sequence_in = []
    for slot in range(4):
        for bits_c in range(2):
            found = jnp.int32(0)
            for bits_f in range(1, 4):
                found = jnp.where(slot_bits[bits_c][bits_f] == slot, bits_f, found)
            sequence_in.append(found * 2 + bits_c)
    own_slot = slot_bits[0][0]

    places = jnp.arange(length, dtype=jnp.int32)
    live_mask = (places < lengths[0]).astype(F32)[:, None]
    upstream_own = (cotangent[0].astype(F32) * live_mask).astype(BF16)
    upstream_blocks = jnp.stack(
        [read for chunk in spread(upstream_own) for read in map(join, chunk)]
    )
    upstream_all = jnp.stack(
        [lax.dynamic_index_in_dim(upstream_blocks, n, 0, keepdims=False) for n in sequence_in]
    )

    tables = rotation_tables(length)
    decay = decay_mask(length, head)
    row_bytes = (length, breadth)
    saved, summed, leaving = None, GroupSum(), [upstream_all]
    token_chunks = spread(tokens[0])
    order = (3, 1, 2, 0)
    for i, n in enumerate(order):
        results = chunk_call(
            mixer_forward,
            "mixer_forward",
            n,
            token_chunks[n],
            [features[:2], tables, decay, mixer_weight, weight_o],
            [],
            saved,
            [
                ((length, breadth), BF16),
                ((length, 2 * KEY + VAL), BF16),
                ((length, VAL), F32),
                ((length, VAL), BF16),
            ],
            [(row_bytes, BF16)] * 2,
            leaving[: max(1, i)] if i < 3 else leaving,
        )
        saved = results[:4]
        leaving.append(summed.terms(n, results[4:6]))
    mixer_normed, qkv_all, gate_all, gated_all = saved
    hidden_state = tokens[0].astype(F32) + summed.total(feed_weight)

    feed_hat, feed_inverse = statistics(hidden_state, EPSILON)
    feed_own = (feed_hat * features[2] + features[3]).astype(BF16)

    def feed_call(n, chunk, earlier):
        return chunk_call(
            feed_forward,
            "feed_forward",
            n,
            chunk,
            [feed_weight],
            [],
            earlier[-1][:3] if earlier else None,
            [((length, breadth), BF16), ((length, hidden), BF16), ((length, 2 * hidden), F32)],
            [((8, 128), F32)],
            [down_weight] if n == 3 else [],
        )

    saved = chunks_in_turn(feed_own, feed_call)[-1][:3]
    feed_normed, activated, slopes = saved
    down_product = dot_rows(
        activated.reshape(GROUP * length, hidden), upstream_all.reshape(GROUP * length, breadth)
    ).astype(BF16)
    down_grad = lax.psum_scatter(down_product, "z", scatter_dimension=0, tiled=True)

    saved, summed, leaving, feed_parts = None, GroupSum(), [down_product], [None] * 4
    for i, n in enumerate(order):
        results = chunk_call(
            feed_backward,
            "feed_backward",
            n,
            [],
            [feed_weight, down_weight],
            [activated, slopes, upstream_all],
            saved,
            [((length, 2 * hidden), BF16)],
            [(row_bytes, BF16)] * 4,
            leaving[: max(1, i)] if i < 3 else leaving,
        )
        saved = results[:1]
        feed_parts[n] = results[1:3]
        leaving.append(summed.terms(n, results[3:5]))
    feed_product = dot_rows(
        feed_normed.reshape(GROUP * length, breadth),
        saved[0].reshape(GROUP * length, -1),
    ).astype(BF16)
    feed_normed_grad = summed.total(feed_product, down_grad)
    feed_gain_part = jnp.sum(feed_normed_grad * feed_hat, axis=0)
    feed_bias_part = jnp.sum(feed_normed_grad, axis=0)
    state_grad = upstream_all[0].astype(F32) + pull_back(
        feed_hat, feed_inverse, feed_normed_grad * features[2]
    )
    own_grad_low = state_grad.astype(BF16)

    def sum_layers(grads):
        return lax.psum_scatter(
            grads.reshape(4, -1, grads.shape[-1]), "z", scatter_dimension=1, tiled=True
        )

    def to_owners(mine):
        return to_members(mine.reshape(GROUP, local_model, -1))

    feed_summed = sum_layers(feed_product)
    feed_grads = to_owners(feed_summed)

    feed_terms, held, leaving = GroupSum(), [], []

    def backward_call(n, chunk, earlier):
        if n == 3:
            held.extend(after([part for pair in feed_parts for part in pair], earlier[1][-1]))
            leaving.append(feed_terms.terms(3, held[6:]))
        return chunk_call(
            mixer_backward,
            "mixer_backward",
            n,
            chunk,
            [tables, decay, mixer_weight, weight_o],
            [qkv_all, gate_all],
            earlier[-1][:3] if earlier else None,
            [((length, breadth), BF16), ((length, 2 * KEY), BF16), ((length, 2 * VAL), BF16)],
            [(row_bytes, BF16)] * 2,
            leaving,
            2 * 10**10,
        )

    results = chunks_in_turn(own_grad_low, backward_call)
    saved = results[-1][:3]
    out_grad, qk_grad, vg_grad = (a.reshape(GROUP * length, -1) for a in saved)
    (qk_grad,) = after([qk_grad], feed_summed)
    leaving = [feed_terms.terms(number, held[2 * number :][:2]) for number in (1, 2)]
    (vg_grad,) = after([vg_grad], *leaving)
    feed_terms.terms(0, held[:2])

    normed_rows = mixer_normed.reshape(GROUP * length, breadth)
    qk_product = dot_rows(normed_rows, qk_grad).astype(BF16)
    vg_product = dot_rows(normed_rows, vg_grad).astype(BF16)
    qk_grads = to_owners(sum_layers(qk_product))
    def head_places(at):
        return [(member, at, member * KEY, KEY) for member in range(GROUP)]

    def value_places(at):
        return [
            (member, at + (c * half_layers + l) * local_value, ((member * half_layers + l) * 2 + c) * local_value, local_value)
            for member in range(GROUP)
            for l in range(half_layers)
            for c in range(2)
        ]

    def hidden_places(at):
        return [
            (f * 2 + c, at + l * local_hidden, ((f * layers + l) * 2 + c) * local_hidden, local_hidden)
            for f in range(4)
            for l in range(layers)
            for c in range(2)
        ]

    query_grad, key_grad = lay_out(qk_grads, [head_places(0), head_places(KEY)])
    feed_gate_grad, feed_up_grad = lay_out(feed_grads, [hidden_places(0), hidden_places(hidden)])
    (out_grad,) = after([out_grad], feed_up_grad, key_grad)
    out_product = dot_rows(gated_all.reshape(GROUP * length, VAL), out_grad).astype(BF16)
    vg_grads = to_owners(sum_layers(vg_product))
    output_grad = lax.psum_scatter(
        to_members(out_product, "core"), "z", scatter_dimension=0, tiled=True
    ).astype(F32)

    slot_out = (hidden_state + feed_terms.total()).astype(BF16)
    half = length // 2
    from_x, from_y = swap(slot_out, "x"), swap(slot_out, "y")
    across = jnp.concatenate(
        after([swap(from_y[:half], "x"), swap(from_x[half:], "y")], vg_grads), axis=0
    )
    reached = jnp.stack([slot_out, from_x, from_y, across])
    chosen = lax.dynamic_index_in_dim(reached, own_slot, 0, keepdims=False)
    out_tokens = (live_mask * chosen.astype(F32)).astype(BF16)

    summed = GroupSum()
    for n in order:
        summed.terms(n, results[n][3:5])
    value_grad, gate_grad = lay_out(vg_grads, [value_places(0), value_places(VAL)])
    mixer_normed_grad = summed.total(out_product, gate_grad)
    mixer_hat, mixer_inverse = statistics(tokens[0].astype(F32), EPSILON)
    mixer_gain_part = jnp.sum(mixer_normed_grad * mixer_hat, axis=0)
    mixer_bias_part = jnp.sum(mixer_normed_grad, axis=0)
    input_grad = (
        state_grad + pull_back(mixer_hat, mixer_inverse, mixer_normed_grad * features[0])
    ).astype(BF16)

    def vector_grads(*grads):
        split = jnp.stack(grads).reshape(len(grads), devices, -1).transpose(1, 0, 2)
        return jnp.sum(to_members(split, EVERY), axis=0)

    vector_sums = vector_grads(mixer_gain_part, mixer_bias_part, feed_gain_part, feed_bias_part)


    return (
        out_tokens[None],
        input_grad[None],
        query_grad,
        key_grad,
        value_grad,
        gate_grad,
        vector_sums[0],
        vector_sums[1],
        output_grad,
        feed_gate_grad,
        feed_up_grad,
        down_grad.astype(F32),
        vector_sums[2],
        vector_sums[3],
    )


def join(pieces):
    return jnp.concatenate(pieces, axis=0) if len(pieces) > 1 else pieces[0]


def solution(mesh):
    layers = mesh.shape["dp"] // 2
    fine = Mesh(mesh.devices.reshape(2, 2, layers, 2), EVERY)
    sequences = P(EVERY, None, None)
    rows = P(EVERY, None)
    vector = P(EVERY)
    in_specs = (
        (sequences, vector, P(), sequences)
        + (rows,) * 4
        + (vector,) * 2
        + (rows,) * 4
        + (vector,) * 2
    )
    out_specs = (sequences,) * 2 + (rows,) * 4 + (vector,) * 2 + (rows,) * 4 + (vector,) * 2
    return jax.shard_map(body, mesh=fine, in_specs=in_specs, out_specs=out_specs, check_vma=False)
```

```python
import math

import jax
import jax.numpy as jnp
from jax import lax
from jax.experimental import pallas as pl
from jax.experimental.pallas import tpu as pltpu
from jax.sharding import Mesh, PartitionSpec as P

HEADS = 8
KEY = 256
VAL = 512
EPSILON = 1e-05
RETAIN_EPSILON = 0.05
SCALE = KEY ** (-0.5)

EVERY = ("y", "x", "z", "core")
MEMBERS = ("y", "x", "core")
GROUP = 8
F32 = jnp.float32
BF16 = jnp.bfloat16


def dot(left, right):
    return jnp.dot(left, right, preferred_element_type=F32)


def dot_rows(left, right):
    return lax.dot_general(left, right, (((0,), (0,)), ((), ())), preferred_element_type=F32)


def dot_back(left, right):
    return lax.dot_general(left, right, (((1,), (1,)), ((), ())), preferred_element_type=F32)


def statistics(field_in, offset):
    centred = field_in - jnp.mean(field_in, axis=-1, keepdims=True)
    inverse = lax.rsqrt(jnp.mean(centred * centred, axis=-1, keepdims=True) + offset)
    return centred * inverse, inverse


def pull_back(hat, inverse, grad):
    return inverse * (
        grad
        - jnp.mean(grad, axis=-1, keepdims=True)
        - hat * jnp.mean(grad * hat, axis=-1, keepdims=True)
    )


def rotation_tables(length):
    half_width = KEY // 2
    columns = jnp.arange(half_width).astype(F32)
    angles = jnp.exp(-math.log(10000.0) * columns / (half_width - 1))
    zeta_scale = (2.0 * columns + 0.4 * KEY) / (1.4 * KEY)
    places = jnp.arange(length).astype(F32)[:, None]
    phases = places * angles[None, :]
    tables = []
    for direction in (1.0, -1.0):
        growth = jnp.exp(direction * places / 512.0 * jnp.log(zeta_scale)[None, :])
        tables += [jnp.cos(phases) * growth, jnp.sin(phases) * growth]
    return jnp.stack(tables)


def decay_mask(length, head):
    log_decay = jnp.log(1.0 - jnp.exp2(-5.0 - head.astype(F32)))
    places = jnp.arange(length)
    distance = (places[:, None] - places[None, :]).astype(F32)
    decayed = jnp.where(distance >= 0.0, jnp.exp(log_decay * jnp.maximum(distance, 0.0)), 0.0)
    return decayed * lax.rsqrt(jnp.sum(decayed, axis=-1, keepdims=True))


def read_rows(refs):
    return jnp.concatenate([ref[...] for ref in refs], axis=0) if len(refs) > 1 else refs[0][...]


def turn(field_in, cosine, sine):
    first, second = field_in[:, : KEY // 2], field_in[:, KEY // 2 :]
    return jnp.concatenate([first * cosine - second * sine, second * cosine + first * sine], axis=1)


def turn_back(field_in, cosine, sine):
    first, second = field_in[:, : KEY // 2], field_in[:, KEY // 2 :]
    return jnp.concatenate([first * cosine + second * sine, second * cosine - first * sine], axis=1)


def whole_spec(array):
    zeros = (0,) * array.ndim
    return pl.BlockSpec(array.shape, lambda i: zeros, pipeline_mode=pl.Buffered(1))


def pair_spec(shape, number):
    return pl.BlockSpec((2,) + shape, lambda i: (number,) + (0,) * len(shape))


def chunk_call(body_fn, name, number, pieces, shared, saved_in, buffers, shapes, parts, tokens=(), flops=0):
    flat = [piece for side in pieces for piece in side]
    counts = [len(side) for side in pieces]
    total = len(flat) + len(shared) + len(saved_in)
    carried = [] if buffers is None else list(buffers)

    def kernel(*refs):
        sides, at = [], 0
        for count in counts:
            sides.append(refs[at : at + count])
            at += count
        body_fn(sides, refs[at : at + len(shared)], refs[at + len(shared) : total], refs[total + len(carried) + len(tokens) :])

    outs = [jax.ShapeDtypeStruct((GROUP,) + shape, dtype) for shape, dtype in shapes]
    outs += [jax.ShapeDtypeStruct(shape, dtype) for shape, dtype in parts]
    operands = [*flat, *shared, *saved_in, *carried, *tokens]
    return pl.pallas_call(
        kernel,
        grid=(1,),
        out_shape=outs,
        in_specs=[whole_spec(o) for o in [*flat, *shared]]
        + [pair_spec(o.shape[1:], number) for o in saved_in]
        + [pl.BlockSpec(memory_space=pl.ANY) for _ in [*carried, *tokens]],
        out_specs=[pair_spec(shape, number) for shape, _ in shapes]
        + [pl.BlockSpec(shape, lambda i: (0, 0)) for shape, _ in parts],
        input_output_aliases={total + i: i for i in range(len(carried))},
        compiler_params=pltpu.CompilerParams(vmem_limit_bytes=56 * 1024 * 1024),
        cost_estimate=pl.CostEstimate(flops=flops, bytes_accessed=0, transcendentals=0),
        name=name,
    )(*operands)


def mixer_forward(sides, shared, saved_in, outs):
    features, tables, decay, weight, weight_o = shared
    normed_out, qkv_out, gate_out, gated_out = outs[:4]
    parts = outs[4:]
    cos_q, sin_q, cos_k, sin_k = (tables[i] for i in range(4))
    for s, side in enumerate(sides):
        hat, _ = statistics(read_rows(side).astype(F32), EPSILON)
        normed = (hat * features[0:1, :] + features[1:2, :]).astype(BF16)
        normed_out[s] = normed
        projected = dot(normed, weight[...])
        query_low = turn(projected[:, :KEY], cos_q, sin_q).astype(BF16)
        key_low = turn(projected[:, KEY : 2 * KEY], cos_k, sin_k).astype(BF16)
        value_low = projected[:, 2 * KEY : 2 * KEY + VAL].astype(BF16)
        gate = projected[:, 2 * KEY + VAL :]
        weighted = dot_back(query_low, key_low) * SCALE * decay[...]
        shaped = weighted * lax.rsqrt(1.0 + jnp.sum(weighted * weighted, axis=-1, keepdims=True))
        retained = dot(shaped.astype(BF16), value_low)
        retained_hat, _ = statistics(retained, RETAIN_EPSILON)
        qkv_out[s, :, :KEY] = query_low
        qkv_out[s, :, KEY : 2 * KEY] = key_low
        qkv_out[s, :, 2 * KEY :] = value_low
        gate_out[s] = gate
        gated = (gate * jax.nn.sigmoid(gate) * retained_hat).astype(BF16)
        gated_out[s] = gated
        parts[s][...] = dot(gated, weight_o[...]).astype(BF16)


def mixer_backward(sides, shared, saved_in, outs):
    tables, decay_ref, weight, weight_o = shared
    qkv, gate_ref = saved_in
    og_out, qk_out, vg_out = outs[:3]
    parts = outs[3:]
    cos_q, sin_q, cos_k, sin_k = (tables[i] for i in range(4))
    decay = decay_ref[...]
    for s, side in enumerate(sides):
        out_grad = read_rows(side)
        og_out[s] = out_grad
        gated_grad = dot_back(out_grad, weight_o[...])
        query_low = qkv[s, :, :KEY]
        key_low = qkv[s, :, KEY : 2 * KEY]
        value_low = qkv[s, :, 2 * KEY :]
        weighted = dot_back(query_low, key_low) * SCALE * decay
        inverse_c = lax.rsqrt(1.0 + jnp.sum(weighted * weighted, axis=-1, keepdims=True))
        shaped_low = (weighted * inverse_c).astype(BF16)
        retained_hat, inverse = statistics(dot(shaped_low, value_low), RETAIN_EPSILON)
        gate = gate_ref[s]
        sig = jax.nn.sigmoid(gate)
        gate_grad = (gated_grad * retained_hat * (sig * (1.0 + gate * (1.0 - sig)))).astype(BF16)
        retained_low = pull_back(retained_hat, inverse, gated_grad * (gate * sig)).astype(BF16)
        value_grad = dot_rows(shaped_low, retained_low).astype(BF16)
        shaped_grad = dot_back(retained_low, value_low)
        row_sum = jnp.sum(shaped_grad * weighted, axis=-1, keepdims=True)
        cubed = inverse_c * inverse_c * inverse_c
        score_grad = (decay * (shaped_grad * inverse_c - weighted * (row_sum * cubed))).astype(BF16)
        query_grad = turn_back(dot(score_grad, key_low) * SCALE, cos_q, sin_q).astype(BF16)
        key_grad = turn_back(dot_rows(score_grad, query_low) * SCALE, cos_k, sin_k).astype(BF16)
        both = jnp.concatenate([query_grad, key_grad], axis=1)
        value_gate = jnp.concatenate([value_grad, gate_grad], axis=1)
        qk_out[s] = both
        vg_out[s] = value_gate
        parts[s][...] = dot_back(jnp.concatenate([both, value_gate], axis=1), weight[...]).astype(BF16)


def feed_forward(sides, shared, saved_in, outs):
    (weight,) = shared
    normed_out, act_out, slopes_out, done = outs
    hidden = act_out.shape[2]
    done[...] = jnp.zeros_like(done)
    for s, side in enumerate(sides):
        normed = read_rows(side)
        normed_out[s] = normed
        pre = dot(normed, weight[...])
        gate_pre, up_pre = pre[:, :hidden], pre[:, hidden:]
        phi = 0.5 * (1.0 + lax.erf(gate_pre * math.sqrt(0.5)))
        gelu = gate_pre * phi
        slope = phi + gate_pre * (jnp.exp(-0.5 * gate_pre * gate_pre) * (1.0 / math.sqrt(2.0 * math.pi)))
        act_out[s] = (gelu * up_pre).astype(BF16)
        slopes_out[s, :, :hidden] = up_pre * slope
        slopes_out[s, :, hidden:] = gelu


def feed_backward(sides, shared, saved_in, outs):
    weight, down = shared
    act_ref, slopes, upstream_ref = saved_in
    pre_out = outs[0]
    feed_parts, normed_parts = outs[1:3], outs[3:5]
    for s in range(2):
        act_grad = dot_back(upstream_ref[s], down[...])
        low = (jnp.concatenate([act_grad, act_grad], axis=1) * slopes[s]).astype(BF16)
        pre_out[s] = low
        normed_parts[s][...] = dot_back(low, weight[...]).astype(BF16)
        feed_parts[s][...] = dot(act_ref[s], down[...]).astype(BF16)


def lay_out(received, places):
    rows = received.shape[1]
    widths = [sum(place[3] for place in listed) for listed in places]
    if any(place[3] % 128 for listed in places for place in listed):
        return [
            jnp.concatenate(
                [received[m, :, a : a + w] for m, a, _, w in sorted(listed, key=lambda place: place[2])], axis=1
            ).astype(F32)
            for listed in places
        ]

    def kernel(block, *outs):
        for out, listed in zip(outs, places):
            for m, a, b, w in listed:
                out[:, b : b + w] = block[m, :, a : a + w].astype(F32)

    return pl.pallas_call(
        kernel,
        out_shape=[jax.ShapeDtypeStruct((rows, width), F32) for width in widths],
        name="lay_out",
    )(received)


def swap(field_in, axis):
    return lax.ppermute(field_in, axis, [(0, 1), (1, 0)])


def swap_both(field_in, axes):
    return lax.ppermute(field_in, axes, [(0, 3), (1, 2), (2, 1), (3, 0)])


def after(values, *tokens):
    anywhere = pl.BlockSpec(memory_space=pl.ANY)
    held = pl.pallas_call(
        lambda *refs: None,
        out_shape=[jax.ShapeDtypeStruct(v.shape, v.dtype) for v in values],
        in_specs=[anywhere] * (len(values) + len(tokens)),
        out_specs=[anywhere] * len(values),
        input_output_aliases={i: i for i in range(len(values))},
        cost_estimate=pl.CostEstimate(flops=0, bytes_accessed=0, transcendentals=0),
        name="after",
    )(*values, *tokens)
    return list(held)


def pair_up(pieces):
    return pieces, [swap(piece, "core") for piece in pieces]


def spread(own):
    half = own.shape[0] // 2
    from_x = swap(own, "x")
    from_y = swap(own, "y")
    upper = swap(from_y[:half], "x")
    lower = swap(from_x[half:], "y")
    return [pair_up(pieces) for pieces in ([own], [from_x], [from_y], [upper, lower])]


def chunks_in_turn(own, call):
    half = own.shape[0] // 2
    lower_x, upper_y = swap(own[half:], "x"), swap(own[:half], "y")
    chunk_own = pair_up([own])
    upper_x, lower_y = swap(own[:half], "x"), swap(own[half:], "y")
    results = [call(0, chunk_own, [])]
    lower_x, upper_y = after([lower_x, upper_y], results[0][-1])
    lower, upper = swap(lower_x, "y"), swap(upper_y, "x")
    upper_x, lower_y = after([upper_x, lower_y], lower_x)
    chunk_x, chunk_y = pair_up([upper_x, lower_x]), pair_up([upper_y, lower_y])
    results.append(call(1, chunk_x, results))
    chunk_across = pair_up(after([upper, lower], results[1][-1]))
    results.append(call(2, chunk_y, results))
    results.append(call(3, chunk_across, results))
    return results


def two_cores(pair):
    return pair[0].astype(F32) + swap(pair[1], "core").astype(F32)


class GroupSum:
    def __init__(self):
        self.passing = self.own = None
        self.arrived = []

    def terms(self, number, pair):
        total = two_cores(pair)
        half = total.shape[0] // 2
        if number == 0:
            self.own = total
            return None
        if number == 3:
            total = total.astype(BF16)
            self.passing = after([swap(total[half:], "y"), swap(total[:half], "x")])
            return total
        margins = ((half, 0), (0, half))[number - 1]
        passed = jnp.pad(self.passing[number - 1], (margins, (0, 0)))
        total = (total + passed.astype(F32)).astype(BF16)
        self.arrived.append(swap(total, ("x", "y")[number - 1]))
        return total

    def total(self, *tokens):
        arrived = after(self.arrived, *tokens) if tokens else self.arrived
        return self.own + arrived[0].astype(F32) + arrived[1].astype(F32)


def body(
    tokens,
    lengths,
    dealing,
    cotangent,
    query_weight,
    key_weight,
    value_weight,
    gate_weight,
    mixer_gain,
    mixer_bias,
    output_weight,
    feed_gate,
    feed_up,
    feed_down,
    feed_gain,
    feed_bias,
):
    _, length, breadth = tokens.shape
    layers = lax.axis_size("z")
    devices = 8 * layers
    local_model = query_weight.shape[0]
    local_hidden = feed_down.shape[0]
    local_value = output_weight.shape[0]
    hidden = local_hidden * layers
    half_layers = layers // 2
    fsdp_index = lax.axis_index("y") * 2 + lax.axis_index("x")
    core = lax.axis_index("core")
    layer = lax.axis_index("z")
    head = fsdp_index * 2 + core

    def to_members(packed, axes=MEMBERS):
        return lax.all_to_all(packed, axes, 0, 0, tiled=True)

    def gather_layers(mine):
        return lax.all_gather(
            mine.reshape(4, 2 * local_model, -1), "z", axis=1, tiled=True
        ).reshape(breadth, -1)

    def value_columns(weight):
        split = weight.reshape(local_model, 4, 2, half_layers, 2, local_value)
        return split.transpose(1, 2, 0, 4, 3, 5).reshape(GROUP, local_model, VAL)

    def head_columns(weight):
        return weight.reshape(local_model, HEADS, KEY).transpose(1, 0, 2)

    def hidden_columns(weight):
        split = weight.reshape(local_model, 4, layers, 2, local_hidden)
        return split.transpose(1, 3, 0, 2, 4).reshape(GROUP, local_model, hidden)

    weight_o = lax.all_gather(output_weight, "z", axis=0, tiled=True)
    mixer_mine = to_members(
        jnp.concatenate(
            [
                head_columns(query_weight),
                head_columns(key_weight),
                value_columns(value_weight),
                value_columns(gate_weight),
            ],
            axis=2,
        )
    )
    mixer_weight = gather_layers(mixer_mine)
    feed_packed = jnp.concatenate([hidden_columns(feed_gate), hidden_columns(feed_up)], axis=2)
    feed_mine = to_members(feed_packed)
    feed_weight = gather_layers(feed_mine)
    down_weight = lax.all_gather(feed_down, "z", axis=0, tiled=True)
    weight_o = to_members(weight_o, "core")

    vectors = jnp.stack([mixer_gain, mixer_bias, feed_gain, feed_bias])
    features = to_members(jnp.broadcast_to(vectors[None], (devices,) + vectors.shape), EVERY)
    features = features.transpose(1, 0, 2).reshape(4, breadth).astype(F32)

    slot_bits = []
    for bits_c in range(2):
        numbers = [
            ((fsdp_index ^ bits_f) * layers + layer) * 2 + (core ^ bits_c) for bits_f in range(4)
        ]
        slot_bits.append([fsdp_index ^ (dealing[n] // (2 * layers)) for n in numbers])
    sequence_in = []
    for slot in range(4):
        for bits_c in range(2):
            found = jnp.int32(0)
            for bits_f in range(1, 4):
                found = jnp.where(slot_bits[bits_c][bits_f] == slot, bits_f, found)
            sequence_in.append(found * 2 + bits_c)
    own_slot = slot_bits[0][0]

    places = jnp.arange(length, dtype=jnp.int32)
    live_mask = (places < lengths[0]).astype(F32)[:, None]
    upstream_own = (cotangent[0].astype(F32) * live_mask).astype(BF16)
    upstream_blocks = jnp.stack(
        [read for chunk in spread(upstream_own) for read in map(join, chunk)]
    )
    upstream_all = jnp.stack(
        [lax.dynamic_index_in_dim(upstream_blocks, n, 0, keepdims=False) for n in sequence_in]
    )

    tables = rotation_tables(length)
    decay = decay_mask(length, head)
    row_bytes = (length, breadth)
    saved, summed, leaving = None, GroupSum(), [upstream_all]
    token_chunks = spread(tokens[0])
    order = (3, 1, 2, 0)
    for i, n in enumerate(order):
        results = chunk_call(
            mixer_forward,
            "mixer_forward",
            n,
            token_chunks[n],
            [features[:2], tables, decay, mixer_weight, weight_o],
            [],
            saved,
            [
                ((length, breadth), BF16),
                ((length, 2 * KEY + VAL), BF16),
                ((length, VAL), F32),
                ((length, VAL), BF16),
            ],
            [(row_bytes, BF16)] * 2,
            leaving[: max(1, i)] if i < 3 else leaving,
        )
        saved = results[:4]
        leaving.append(summed.terms(n, results[4:6]))
    mixer_normed, qkv_all, gate_all, gated_all = saved
    hidden_state = tokens[0].astype(F32) + summed.total(feed_weight)

    feed_hat, feed_inverse = statistics(hidden_state, EPSILON)
    feed_own = (feed_hat * features[2] + features[3]).astype(BF16)

    def feed_call(n, chunk, earlier):
        return chunk_call(
            feed_forward,
            "feed_forward",
            n,
            chunk,
            [feed_weight],
            [],
            earlier[-1][:3] if earlier else None,
            [((length, breadth), BF16), ((length, hidden), BF16), ((length, 2 * hidden), F32)],
            [((8, 128), F32)],
            [down_weight] if n == 3 else [],
        )

    saved = chunks_in_turn(feed_own, feed_call)[-1][:3]
    feed_normed, activated, slopes = saved
    down_product = dot_rows(
        activated.reshape(GROUP * length, hidden), upstream_all.reshape(GROUP * length, breadth)
    ).astype(BF16)
    down_grad = lax.psum_scatter(down_product, "z", scatter_dimension=0, tiled=True)

    saved, summed, leaving, feed_parts = None, GroupSum(), [down_product], [None] * 4
    for i, n in enumerate(order):
        results = chunk_call(
            feed_backward,
            "feed_backward",
            n,
            [],
            [feed_weight, down_weight],
            [activated, slopes, upstream_all],
            saved,
            [((length, 2 * hidden), BF16)],
            [(row_bytes, BF16)] * 4,
            leaving[: max(1, i)] if i < 3 else leaving,
        )
        saved = results[:1]
        feed_parts[n] = results[1:3]
        leaving.append(summed.terms(n, results[3:5]))
    feed_product = dot_rows(
        feed_normed.reshape(GROUP * length, breadth),
        saved[0].reshape(GROUP * length, -1),
    ).astype(BF16)
    feed_normed_grad = summed.total(feed_product, down_grad)
    feed_gain_part = jnp.sum(feed_normed_grad * feed_hat, axis=0)
    feed_bias_part = jnp.sum(feed_normed_grad, axis=0)
    state_grad = upstream_all[0].astype(F32) + pull_back(
        feed_hat, feed_inverse, feed_normed_grad * features[2]
    )
    own_grad_low = state_grad.astype(BF16)

    def sum_layers(grads):
        return lax.psum_scatter(
            grads.reshape(4, -1, grads.shape[-1]), "z", scatter_dimension=1, tiled=True
        )

    def to_owners(mine):
        return to_members(mine.reshape(GROUP, local_model, -1))

    feed_summed = sum_layers(feed_product)
    feed_grads = to_owners(feed_summed)

    feed_terms, held, leaving = GroupSum(), [], []

    def backward_call(n, chunk, earlier):
        if n == 3:
            held.extend(after([part for pair in feed_parts for part in pair], earlier[1][-1]))
            leaving.append(feed_terms.terms(3, held[6:]))
        return chunk_call(
            mixer_backward,
            "mixer_backward",
            n,
            chunk,
            [tables, decay, mixer_weight, weight_o],
            [qkv_all, gate_all],
            earlier[-1][:3] if earlier else None,
            [((length, breadth), BF16), ((length, 2 * KEY), BF16), ((length, 2 * VAL), BF16)],
            [(row_bytes, BF16)] * 2,
            leaving,
            2 * 10**10,
        )

    results = chunks_in_turn(own_grad_low, backward_call)
    saved = results[-1][:3]
    out_grad, qk_grad, vg_grad = (a.reshape(GROUP * length, -1) for a in saved)
    (qk_grad,) = after([qk_grad], feed_summed)
    leaving = [feed_terms.terms(number, held[2 * number :][:2]) for number in (1, 2)]
    (vg_grad,) = after([vg_grad], *leaving)
    feed_terms.terms(0, held[:2])

    normed_rows = mixer_normed.reshape(GROUP * length, breadth)
    qk_product = dot_rows(normed_rows, qk_grad).astype(BF16)
    vg_product = dot_rows(normed_rows, vg_grad).astype(BF16)
    qk_grads = to_owners(sum_layers(qk_product))
    def head_places(at):
        return [(member, at, member * KEY, KEY) for member in range(GROUP)]

    def value_places(at):
        return [
            (member, at + (c * half_layers + l) * local_value, ((member * half_layers + l) * 2 + c) * local_value, local_value)
            for member in range(GROUP)
            for l in range(half_layers)
            for c in range(2)
        ]

    def hidden_places(at):
        return [
            (f * 2 + c, at + l * local_hidden, ((f * layers + l) * 2 + c) * local_hidden, local_hidden)
            for f in range(4)
            for l in range(layers)
            for c in range(2)
        ]

    query_grad, key_grad = lay_out(qk_grads, [head_places(0), head_places(KEY)])
    feed_gate_grad, feed_up_grad = lay_out(feed_grads, [hidden_places(0), hidden_places(hidden)])
    (out_grad,) = after([out_grad], feed_up_grad, key_grad)
    out_product = dot_rows(gated_all.reshape(GROUP * length, VAL), out_grad).astype(BF16)
    vg_grads = to_owners(sum_layers(vg_product))
    output_grad = lax.psum_scatter(
        to_members(out_product, "core"), "z", scatter_dimension=0, tiled=True
    ).astype(F32)

    slot_out = (hidden_state + feed_terms.total()).astype(BF16)
    half = length // 2
    from_x, from_y = swap(slot_out, "x"), swap(slot_out, "y")
    across = jnp.concatenate(
        after([swap(from_y[:half], "x"), swap(from_x[half:], "y")], vg_grads), axis=0
    )
    reached = jnp.stack([slot_out, from_x, from_y, across])
    chosen = lax.dynamic_index_in_dim(reached, own_slot, 0, keepdims=False)
    out_tokens = (live_mask * chosen.astype(F32)).astype(BF16)

    summed = GroupSum()
    for n in order:
        summed.terms(n, results[n][3:5])
    mixer_normed_grad = summed.total(out_product, vg_grads)
    value_grad, gate_grad = lay_out(vg_grads, [value_places(0), value_places(VAL)])
    mixer_hat, mixer_inverse = statistics(tokens[0].astype(F32), EPSILON)
    mixer_gain_part = jnp.sum(mixer_normed_grad * mixer_hat, axis=0)
    mixer_bias_part = jnp.sum(mixer_normed_grad, axis=0)
    input_grad = (
        state_grad + pull_back(mixer_hat, mixer_inverse, mixer_normed_grad * features[0])
    ).astype(BF16)

    def vector_grads(*grads):
        split = jnp.stack(grads).reshape(len(grads), devices, -1).transpose(1, 0, 2)
        return jnp.sum(to_members(split, EVERY), axis=0)

    vector_sums = vector_grads(mixer_gain_part, mixer_bias_part, feed_gain_part, feed_bias_part)


    return (
        out_tokens[None],
        input_grad[None],
        query_grad,
        key_grad,
        value_grad,
        gate_grad,
        vector_sums[0],
        vector_sums[1],
        output_grad,
        feed_gate_grad,
        feed_up_grad,
        down_grad.astype(F32),
        vector_sums[2],
        vector_sums[3],
    )


def join(pieces):
    return jnp.concatenate(pieces, axis=0) if len(pieces) > 1 else pieces[0]


def solution(mesh):
    layers = mesh.shape["dp"] // 2
    fine = Mesh(mesh.devices.reshape(2, 2, layers, 2), EVERY)
    sequences = P(EVERY, None, None)
    rows = P(EVERY, None)
    vector = P(EVERY)
    in_specs = (
        (sequences, vector, P(), sequences)
        + (rows,) * 4
        + (vector,) * 2
        + (rows,) * 4
        + (vector,) * 2
    )
    out_specs = (sequences,) * 2 + (rows,) * 4 + (vector,) * 2 + (rows,) * 4 + (vector,) * 2
    return jax.shard_map(body, mesh=fine, in_specs=in_specs, out_specs=out_specs, check_vma=False)
```
